32 devices in a mesh: slab: 8 (over z, x), head: 4 (over y, core).
Axes of the slice: x: 2, y: 2, z: 4, core: 2. Of those that a mesh axis runs over, the one named last changes fastest.
Arguments:
- atom_feats: bfloat16 [2, 4096, 128], P(None, 'slab'), may hold values from -16 to 16
- pair_feats: bfloat16 [4096, 16, 128], P('slab'), may hold values from -8 to 330
- tok_slot: int32 [4096], P('slab'), may hold values from 0 to 255, as said below
- w_proj: bfloat16 [4, 128, 128], P(None, None, 'head'), may hold values from -0.5 to 0.5
- w_out: bfloat16 [128, 128], P('head'), may hold values from -0.5 to 0.5
- w_pair: bfloat16 [16, 4], P(None, 'head'), may hold values from -1.2 to 1.2
- w_tok: bfloat16 [128, 768], P(None, 'head'), may hold values from -0.5 to 0.5
- d_tok: bfloat16 [2, 256, 768], P(None, 'slab', 'head'), may hold values from -6 to 6
Outputs:
- tok_act: bfloat16 [2, 256, 768], P(None, 'slab', 'head')
- grad_proj: float32 [4, 128, 128], P(None, None, 'head')
- grad_out: float32 [128, 128], P('head')
- grad_pair: float32 [16, 4], P(None, 'head')
- grad_tok: float32 [128, 768], P(None, 'head')
The draws below stay inside these ranges and needn't reach their ends.
Inputs may be any that keep to these rules, and one draw needn't show every extreme that they name: `tok_slot`: never falling. The atoms s * 512 to (s + 1) * 512 - 1 use slots s * 32 to s * 32 + n - 1, each at least once, with n from 16 to 32; the first of these atoms is in slot s * 32. The last slab and one other use all 32 slots.
All inputs are finite; a program needn't handle non-finite values.
Results may differ from the reference program's by a relative error of at most 0.023.
Values may be sent and summed in bfloat16 or wider, within the bound.
A program may use at most 64 MiB of HBM per device.

```python
import math
import jax
import jax.numpy as jnp
from jax import lax

ATOM_W = 128
TOKEN_W = 768
HEADS = 4
HEAD_FEATURES = 32
PAIR_C = 16
Q_WIN = 32
K_WIN = 128
RIM = 48
SAMPLES = 2
ATOM_DEV = 512
TOK_CAP = 32
ATOM_TOTAL = 4096
TOKENS = 256


def draw_atom_feats(key, part):
    key_list = jax.random.split(key, 3)
    spread = math.log(10.0)
    row_scale = jnp.exp(jax.random.uniform(key_list[1], (1, ATOM_TOTAL, 1)) * spread) / 10.0 ** 0.5
    column_scale = jnp.exp(jax.random.uniform(key_list[2], (1, 1, ATOM_W)) * spread) / 10.0 ** 0.5
    values = jax.random.normal(key_list[0], (SAMPLES, ATOM_TOTAL, ATOM_W)) * row_scale * column_scale
    return jnp.clip(values, -16.0, 16.0).astype(jnp.bfloat16)


def draw_pair_feats(key, part):
    key_list = jax.random.split(key, 1)
    values = jax.random.normal(key_list[0], (ATOM_TOTAL, PAIR_C, K_WIN))
    return jnp.clip(values, -8.0, 330.0).astype(jnp.bfloat16)


def draw_w_pair(key, part):
    key_list = jax.random.split(key, 2)
    values = jax.random.normal(key_list[0], (PAIR_C, HEADS)) * PAIR_C ** (-0.5)
    leading = jax.random.uniform(key_list[1], (1, HEADS), minval=0.8, maxval=1.2)
    channel = jnp.arange(PAIR_C, dtype=jnp.int32)[:, None]
    values = jnp.where(channel == 0, leading, values)
    return jnp.clip(values, -1.2, 1.2).astype(jnp.bfloat16)


def draw_tok_slot(key, part):
    slab_total = ATOM_TOTAL // ATOM_DEV
    key_list = jax.random.split(key, 3)
    used = jax.random.randint(key_list[0], (slab_total,), TOK_CAP // 2, TOK_CAP + 1)
    full_slab = jax.random.randint(key_list[1], (), 0, slab_total)
    slab_ids = jnp.arange(slab_total, dtype=jnp.int32)
    used = jnp.where((slab_ids == full_slab) | (slab_ids == slab_total - 1), TOK_CAP, used)
    order = jax.vmap(lambda sub_key: jax.random.permutation(sub_key, ATOM_DEV))(jax.random.split(key_list[2], slab_total))
    order = order.astype(jnp.int32)
    first_value = order[:, :1]
    order = jnp.where(order == 0, first_value, order)
    order = order.at[:, 0].set(0)
    starts = (order < used[:, None]).astype(jnp.int32)
    ranking = jnp.cumsum(starts, axis=1)
    slots = slab_ids[:, None] * TOK_CAP + ranking - 1
    return slots.reshape(-1).astype(jnp.int32)


def levels(stream_key, extent, cuts, smallest, high):
    loudness, own = 1.0, jax.random.fold_in(stream_key, 6)
    for axis_at, shards_of in cuts:
        draws = jnp.exp(jax.random.uniform(jax.random.fold_in(own, axis_at), (shards_of,), jnp.float32, smallest / len(cuts), high / len(cuts)))
        loudness = loudness * jnp.repeat(draws, extent[axis_at] // shards_of).reshape([-1 if axis == axis_at else 1 for axis in range(len(extent))])
    return loudness


def gaussian(rng, extent, width, reach, shards=(), kind=jnp.bfloat16):
    entries = width * jax.random.normal(rng, extent, jnp.float32)
    if shards:
        entries = entries * levels(rng, extent, shards, -0.22, 0.18)
    return jnp.clip(entries, -reach, reach).astype(kind)


def setup_inputs(seed: int = 0) -> dict:
    seeds = jax.random.split(jax.random.key(seed), 9)
    atom_feats = draw_atom_feats(jax.random.fold_in(seeds[8], 71), 0)
    pair_feats = draw_pair_feats(jax.random.fold_in(seeds[8], 71), 0)
    tok_slot = draw_tok_slot(jax.random.fold_in(seeds[8], 71), 0)
    w_proj = gaussian(seeds[3], (4, ATOM_W, HEADS * HEAD_FEATURES), ATOM_W ** -0.5, 0.5, ((2, 4),))
    w_out = gaussian(seeds[4], (HEADS * HEAD_FEATURES, ATOM_W), (HEADS * HEAD_FEATURES) ** -0.5, 0.5, ((0, 4),))
    w_pair = draw_w_pair(jax.random.fold_in(seeds[8], 71), 0)
    w_tok = gaussian(seeds[6], (ATOM_W, TOKEN_W), ATOM_W ** -0.5, 0.5, ((1, 4),))
    d_tok = gaussian(seeds[7], (SAMPLES, TOKENS, TOKEN_W), 1.0, 6.0, ((1, 8), (2, 4)))
    return {"atom_feats": atom_feats, "pair_feats": pair_feats, "tok_slot": tok_slot, "w_proj": w_proj, "w_out": w_out, "w_pair": w_pair, "w_tok": w_tok, "d_tok": d_tok}


EPSILON = 1e-05

def key_windows(extended, block_count):
    row_total = block_count * Q_WIN
    pieces = []
    for offset in range(K_WIN // Q_WIN):
        segment = extended[Q_WIN * offset:Q_WIN * offset + row_total]
        pieces.append(segment.reshape((block_count, Q_WIN) + extended.shape[1:]))
    return jnp.concatenate(pieces, axis=1)

def key_unwindowed_rows(windowed, block_count):
    row_total = block_count * Q_WIN
    margin = K_WIN - Q_WIN
    summed = None
    for offset in range(K_WIN // Q_WIN):
        segment = windowed[:, Q_WIN * offset:Q_WIN * (offset + 1)].reshape((row_total,) + windowed.shape[2:])
        segment = jnp.pad(segment, ((Q_WIN * offset, margin - Q_WIN * offset), (0, 0)))
        summed = segment if summed is None else summed + segment
    return summed[RIM:RIM + row_total]

def reference(atom_feats, pair_feats, tok_slot, w_proj, w_out, w_pair, w_tok, d_tok):
    block_count = ATOM_TOTAL // Q_WIN
    score_scale = HEAD_FEATURES ** (-0.5)
    factor = (SAMPLES * ATOM_TOTAL) ** (-0.5)
    group_width = TOKEN_W // HEADS
    positions = Q_WIN * jnp.arange(block_count, dtype=jnp.int32)[:, None] - RIM + jnp.arange(K_WIN, dtype=jnp.int32)[None, :]
    in_range = (positions >= 0) & (positions < ATOM_TOTAL)
    pair_bias_terms = jnp.einsum('icj,ch->hij', pair_feats.astype(jnp.float32), w_pair.astype(jnp.float32))
    pair_bias_terms = pair_bias_terms.reshape(HEADS, block_count, Q_WIN, K_WIN)
    counts = jax.ops.segment_sum(jnp.ones((ATOM_TOTAL,), jnp.float32), tok_slot, TOKENS)
    divisor = jnp.maximum(counts, 1.0)

    def one_sample(running, inputs):
        grad_proj, grad_out, grad_tok, bias_sum = running
        sample_feats, sample_cot = inputs
        feats_float = sample_feats.astype(jnp.float32)
        centered = feats_float - lax.optimization_barrier(jnp.mean(feats_float, axis=1, keepdims=True))
        variance = lax.optimization_barrier(jnp.mean(centered * centered, axis=1, keepdims=True))
        normed = (centered * lax.rsqrt(variance + EPSILON)).astype(jnp.bfloat16)
        projected = [jnp.dot(normed, w_proj[which], preferred_element_type=jnp.float32) for which in range(4)]
        queries = (projected[0] * score_scale).astype(jnp.bfloat16)
        keys_all = projected[1].astype(jnp.bfloat16)
        values_all = projected[2].astype(jnp.bfloat16)
        gating = jax.nn.sigmoid(projected[3])
        attn_sum = jnp.zeros((ATOM_TOTAL, ATOM_W), jnp.float32)
        kept_state = []
        for head_position in range(HEADS):
            columns = slice(head_position * HEAD_FEATURES, (head_position + 1) * HEAD_FEATURES)
            query_block_rows = queries[:, columns].astype(jnp.float32).reshape(block_count, Q_WIN, HEAD_FEATURES)
            key_window_rows = key_windows(jnp.pad(keys_all[:, columns], ((RIM, RIM), (0, 0))), block_count).astype(jnp.float32)
            value_window_rows = key_windows(jnp.pad(values_all[:, columns], ((RIM, RIM), (0, 0))), block_count).astype(jnp.float32)
            attention_scores = jnp.einsum('yeh,yjh->yej', query_block_rows, key_window_rows) + pair_bias_terms[head_position]
            attention_scores = jnp.where(in_range[:, None, :], attention_scores, -jnp.inf)
            highest = lax.optimization_barrier(jnp.max(attention_scores, axis=2, keepdims=True))
            exponent = jnp.exp(attention_scores - highest)
            attn_weights = exponent / lax.optimization_barrier(jnp.sum(exponent, axis=2, keepdims=True))
            weight_half_precision = attn_weights.astype(jnp.bfloat16)
            attended_output = jnp.einsum('mxh,mhr->mxr', weight_half_precision.astype(jnp.float32), value_window_rows).reshape(ATOM_TOTAL, HEAD_FEATURES)
            heads_out = (gating[:, columns] * attended_output).astype(jnp.bfloat16)
            head_part = jnp.dot(heads_out, w_out[columns], preferred_element_type=jnp.float32)
            attn_sum = attn_sum + lax.optimization_barrier(head_part.astype(jnp.bfloat16)).astype(jnp.float32)
            kept_state.append((query_block_rows, key_window_rows, value_window_rows, attn_weights, weight_half_precision, attended_output, heads_out))
        mixed_half = (feats_float + attn_sum).astype(jnp.bfloat16)
        pre_act = jnp.dot(mixed_half, w_tok, preferred_element_type=jnp.float32)
        act_gate = jax.nn.sigmoid(pre_act)
        atom_act = (pre_act * act_gate).astype(jnp.bfloat16)
        token_sums = jax.ops.segment_sum(atom_act.astype(jnp.float32), tok_slot, TOKENS)
        tok_act = (token_sums / divisor[:, None]).astype(jnp.bfloat16)
        tok_grad = (sample_cot.astype(jnp.float32) / divisor[:, None]).astype(jnp.bfloat16)
        slope = act_gate * (1.0 + pre_act * (1.0 - act_gate))
        act_grad = (tok_grad[tok_slot].astype(jnp.float32) * slope).astype(jnp.bfloat16)
        grad_tok = grad_tok + jnp.dot(mixed_half.T, act_grad, preferred_element_type=jnp.float32)
        mixed_total = jnp.zeros((ATOM_TOTAL, ATOM_W), jnp.float32)
        for head_position in range(HEADS):
            columns = slice(head_position * group_width, (head_position + 1) * group_width)
            head_part = jnp.dot(act_grad[:, columns], w_tok[:, columns].T, preferred_element_type=jnp.float32)
            mixed_total = mixed_total + lax.optimization_barrier(head_part.astype(jnp.bfloat16)).astype(jnp.float32)
        mixed_grad = mixed_total.astype(jnp.bfloat16)
        for head_position in range(HEADS):
            columns = slice(head_position * HEAD_FEATURES, (head_position + 1) * HEAD_FEATURES)
            query_block_rows, key_window_rows, value_window_rows, attn_weights, weight_half_precision, attended_output, heads_out = kept_state[head_position]
            head_gate = gating[:, columns]
            out_grad = jnp.dot(mixed_grad, w_out[columns].T, preferred_element_type=jnp.float32)
            grad_out = grad_out.at[columns].add(jnp.dot(heads_out.T, mixed_grad, preferred_element_type=jnp.float32))
            att_grad = (head_gate * out_grad).astype(jnp.bfloat16)
            gate_grad = (out_grad * attended_output * head_gate * (1.0 - head_gate)).astype(jnp.bfloat16)
            attention_block_rows = att_grad.astype(jnp.float32).reshape(block_count, Q_WIN, HEAD_FEATURES)
            probability_gradient = jnp.einsum('yeh,yjh->yej', attention_block_rows, value_window_rows)
            score_grad = attn_weights * (probability_gradient - lax.optimization_barrier(jnp.sum(attn_weights * probability_gradient, axis=2, keepdims=True)))
            score_single_precision = score_grad.astype(jnp.bfloat16).astype(jnp.float32)
            query_gradient = (score_scale * jnp.einsum('mxh,mhr->mxr', score_single_precision, key_window_rows)).reshape(ATOM_TOTAL, HEAD_FEATURES).astype(jnp.bfloat16)
            key_gradient = key_unwindowed_rows(jnp.einsum('gys,gyp->gsp', score_single_precision, query_block_rows), block_count).astype(jnp.bfloat16)
            value_gradient = key_unwindowed_rows(jnp.einsum('gys,gyp->gsp', weight_half_precision.astype(jnp.float32), attention_block_rows), block_count).astype(jnp.bfloat16)
            for which, grad_part in enumerate((query_gradient, key_gradient, value_gradient, gate_grad)):
                grad_proj = grad_proj.at[which, :, columns].add(jnp.dot(normed.T, grad_part, preferred_element_type=jnp.float32))
            bias_sum = bias_sum.at[head_position].add(score_single_precision.reshape(ATOM_TOTAL, K_WIN))
        return ((grad_proj, grad_out, grad_tok, bias_sum), tok_act)
    initial = (jnp.zeros((4, ATOM_W, HEADS * HEAD_FEATURES), jnp.float32), jnp.zeros((HEADS * HEAD_FEATURES, ATOM_W), jnp.float32), jnp.zeros((ATOM_W, TOKEN_W), jnp.float32), jnp.zeros((HEADS, ATOM_TOTAL, K_WIN), jnp.float32))
    totals, tok_act = lax.scan(one_sample, initial, (atom_feats, d_tok))
    grad_proj, grad_out, grad_tok, bias_sum = totals
    bias_grad = lax.optimization_barrier(bias_sum.astype(jnp.bfloat16)).astype(jnp.float32)
    grad_pair = jnp.einsum('icj,hij->ch', pair_feats.astype(jnp.float32), bias_grad)
    return (tok_act, grad_proj * factor, grad_out * factor, grad_pair * factor, grad_tok * factor)
```

```python
import functools
import jax
import jax.numpy as jnp
from jax import lax
from jax.experimental import pallas as pl
from jax.experimental.pallas import tpu as pltpu
from jax.sharding import PartitionSpec as P

Q_WIN = 32
K_WIN = 128
RIM = 48
EPSILON = 1e-05
MASKED = -1e30
BF = jnp.bfloat16
F32 = jnp.float32
NT = (((1,), (1,)), ((), ()))
NN = (((1,), (0,)), ((), ()))
TN = (((0,), (0,)), ((), ()))


def mm(a, b, dims=NN):
    return lax.dot_general(a, b, dims, preferred_element_type=F32)


def iota(shape, dim):
    return lax.broadcasted_iota(jnp.int32, shape, dim)


def layer_norm(x):
    x = x.astype(F32)
    centered = x - jnp.mean(x, axis=-1, keepdims=True)
    variance = jnp.mean(centered * centered, axis=-1, keepdims=True)
    return (centered * lax.rsqrt(variance + EPSILON)).astype(BF)


def kernel(
    n, heads, inner,
    feats_in, pair_in, slot_in, wproj_in, wout_in, wpair_in, wtok_in, dtok_in,
    tok_out, gproj_out, gout_out, gpair_out, gtok_out,
    fx, pair, slot, slot_own, wproj, wout, wpair, wtok, dtok,
    keyed, bias, mixer, queries, gate, mq, prob, zcat, att, hb, half, tg, spread, acts, ags, mg, attg, ma, qg, ycat, dcat,
    tsend, trecv, eh, ehr, ebuf, erecv, eres, lh, lhr, lbuf, lrecv, lres, xbuf,
    in_sem, pair_sem, w_sem, halo_sem, t_sem, eh_sem, e_sem, eg_sem, lh_sem, l_sem, lg_sem, x_sem,
):
    samples = fx.shape[0]
    width = fx.shape[2]
    atoms = fx.shape[1] - 2 * RIM
    depth = wproj.shape[2]
    own_atoms = atoms // heads
    blocks = own_atoms // Q_WIN
    rows = samples * own_atoms
    reach = own_atoms + 2 * RIM
    slots, token_cols = dtok.shape[2], dtok.shape[3]
    channels = wpair.shape[2]
    flat = Q_WIN * channels
    stack = heads * Q_WIN
    scale = depth ** (-0.5)
    factor = (samples * atoms * n) ** (-0.5)
    outer = n // inner
    me_s = lax.axis_index("slab")
    me_h = lax.axis_index("head")
    own = lax.rem(me_s, inner)
    base = me_s - own
    sends = []

    def head_peer(k):
        return {"head": lax.rem(me_h + k, heads)}

    def inner_peer(k):
        return {"slab": base + lax.rem(own + k, inner)}

    def outer_peer(k):
        return {"slab": lax.rem(me_s + k * inner, n)}

    def ring_peer(k):
        return {"slab": lax.rem(me_s + k + n, n)}

    def send(src, dst, sems, index, device):
        copy = pltpu.make_async_remote_copy(
            src_ref=src, dst_ref=dst, send_sem=sems.at[(0,) + index], recv_sem=sems.at[(1,) + index],
            device_id=device, device_id_type=pl.DeviceIdType.MESH,
        )
        copy.start()
        sends.append(copy)
        return copy

    greeted = [head_peer(k) for k in range(1, heads)] + [inner_peer(k) for k in range(1, inner)]
    greeted += [outer_peer(k) for k in range(1, outer)]
    if outer > 1:
        greeted += [ring_peer(1), ring_peer(-1)]
    barrier = pltpu.get_barrier_semaphore()
    for device in greeted:
        pl.semaphore_signal(barrier, inc=1, device_id=device, device_id_type=pl.DeviceIdType.MESH)

    first_atom = pl.multiple_of(me_h * own_atoms, own_atoms)
    loads = [
        pltpu.make_async_copy(a, b, in_sem.at[i])
        for i, (a, b) in enumerate(
            [
                (feats_in, fx.at[:, RIM : RIM + atoms, :]),
                (wproj_in, wproj.at[:, me_h]),
                (wout_in, wout.at[me_h]),
                (slot_in, slot),
                (slot_in.at[:, pl.ds(first_atom, own_atoms)], slot_own),
                (dtok_in, dtok.at[me_h]),
                (wpair_in, wpair.at[me_h]),
                (wtok_in, wtok.at[me_h]),
            ]
        )
    ]
    pair_loads = [
        pltpu.make_async_copy(
            pair_in.at[pl.ds(pl.multiple_of(first_atom * channels, flat) + b * flat, flat), :],
            pair.at[:, b * K_WIN : (b + 1) * K_WIN],
            pair_sem.at[b],
        )
        for b in range(blocks)
    ]
    for load in loads + pair_loads:
        load.start()

    pl.semaphore_wait(barrier, len(greeted))

    far_first = [heads // 2] + [k for k in range(1, heads) if k != heads // 2]
    shared = (
        (wproj_in, lambda: wproj.at[:, me_h]),
        (wpair_in, lambda: wpair.at[me_h]),
        (wout_in, lambda: wout.at[me_h]),
        (wtok_in, lambda: wtok.at[me_h]),
        (dtok_in, lambda: dtok.at[me_h]),
    )
    shares = []
    for i, (src, dst) in enumerate(shared):
        shares.append([send(src, dst(), w_sem, (i, k - 1), head_peer(k)) for k in far_first])
        if i == 1:
            to_left = send(
                feats_in.at[:, 0:RIM, :], fx.at[:, RIM + atoms : RIM + atoms + RIM, :], halo_sem, (1,), ring_peer(-1)
            )
            to_right = send(feats_in.at[:, atoms - RIM : atoms, :], fx.at[:, 0:RIM, :], halo_sem, (0,), ring_peer(1))

    def arrive(i):
        for copy in shares[i]:
            copy.wait_recv()

    lane_group = iota((Q_WIN, width), 1) // depth

    def diagonal_pick(tall):
        out = tall[0:Q_WIN]
        for h in range(1, heads):
            out = jnp.where(lane_group == h, tall[h * Q_WIN : (h + 1) * Q_WIN], out)
        return out

    def masked_stack(wide):
        return jnp.concatenate([jnp.where(lane_group == h, wide, 0.0) for h in range(heads)], axis=0).astype(BF)

    def feats_rows(s, start, size):
        return fx[s, pl.ds(first_atom + start, size), :]

    loads[0].wait()
    for s in range(samples):
        keyed[s, RIM : RIM + own_atoms, width : 2 * width] = layer_norm(feats_rows(s, RIM, own_atoms))

    loads[3].wait()
    loads[4].wait()
    slot_ids = me_s * slots
    member = jnp.where(slot[...] == slot_ids + iota((slots, atoms), 0), 1.0, 0.0)
    divisor = jnp.maximum(jnp.sum(member, axis=1, keepdims=True), 1.0)
    member = jnp.where(slot_own[...] == slot_ids + iota((slots, own_atoms), 0), 1.0, 0.0).astype(BF)

    loads[1].wait()
    arrive(0)
    own_normed = jnp.concatenate(
        [keyed[s, RIM : RIM + own_atoms, width : 2 * width] for s in range(samples)], axis=0
    )
    projected = mm(own_normed, wproj[0].reshape(heads * depth, width), NT) * scale
    queries[...] = projected.astype(BF)
    for s in range(samples):
        for b in range(blocks):
            at = s * own_atoms + b * Q_WIN
            mq[s * blocks + b] = masked_stack(queries[at : at + Q_WIN, :].astype(F32))
    gate[...] = jax.nn.sigmoid(mm(own_normed, wproj[3].reshape(heads * depth, width), NT))

    to_right.wait_recv()
    to_left.wait_recv()
    key_value = wproj[1:3].reshape(2 * heads * depth, width)
    for s in range(samples):
        for start in (0, RIM + own_atoms):
            keyed[s, start : start + RIM, width : 2 * width] = layer_norm(feats_rows(s, start, RIM))
        both = mm(keyed[s, :, width : 2 * width], key_value, NT).astype(BF)
        keyed[s, :, 0:width] = both[:, 0:width]
        keyed[s, :, 2 * width : 3 * width] = both[:, width : 2 * width]

    loads[6].wait()
    arrive(1)
    picker = lax.rem(iota((channels, flat), 1), channels) == iota((channels, flat), 0)
    w_tall = jnp.concatenate(
        [jnp.broadcast_to(wpair[h].astype(F32), (Q_WIN, channels)) for h in range(heads)], axis=0
    ).astype(BF)
    w_rows = mm(w_tall, picker.astype(F32).astype(BF))
    diagonal = iota((stack, flat), 1) // channels == lax.rem(iota((stack, flat), 0), Q_WIN)
    mixer[...] = jnp.where(diagonal, w_rows, 0.0).astype(BF)
    for load in pair_loads:
        load.wait()
    block_start = (me_s * heads + me_h) * own_atoms - RIM
    for b in range(blocks):
        where = block_start + b * Q_WIN + iota((stack, K_WIN), 1)
        inside = (where >= 0) & (where < atoms * n)
        cols = slice(b * K_WIN, (b + 1) * K_WIN)
        bias[:, cols] = jnp.where(inside, mm(mixer[...], pair[:, cols]), MASKED)

    def window(s, b, first, last):
        return keyed[s, b * Q_WIN : b * Q_WIN + K_WIN, first * width : last * width]

    tiles = [(s, b) for s in range(samples) for b in range(blocks)]

    for s, b in tiles:
        t = s * blocks + b
        at = slice(s * own_atoms + b * Q_WIN, s * own_atoms + (b + 1) * Q_WIN)
        scores = mm(mq[t], window(s, b, 0, 1), NT) + bias[:, b * K_WIN : (b + 1) * K_WIN]
        top = jnp.max(scores, axis=1, keepdims=True)
        e = jnp.exp(scores - top)
        p = e * (1.0 / jnp.sum(e, axis=1, keepdims=True))
        prob[t] = p
        mixed_values = mm(p.astype(BF), window(s, b, 1, 3))
        for h in range(heads):
            zcat[at, h * width : (h + 1) * width] = mixed_values[h * Q_WIN : (h + 1) * Q_WIN, 0:width].astype(BF)
        attended = diagonal_pick(mixed_values[:, width : 2 * width])
        att[at, :] = attended
        hb[at, :] = (gate[at, :] * attended).astype(BF)

    loads[5].wait()
    arrive(4)
    for s in range(samples):
        wide = jnp.concatenate([dtok[h, s].astype(F32) for h in range(heads)], axis=1)
        tg[s] = (wide / divisor).astype(BF)
        spread[s * own_atoms : (s + 1) * own_atoms, :] = mm(member, tg[s], TN).astype(BF)

    loads[2].wait()
    arrive(2)
    w_out = wout[...].reshape(heads * depth, width)
    loads[7].wait()
    arrive(3)
    w_tok = wtok.reshape(heads * token_cols, width)
    mixed = mm(hb[...], w_out)
    residual = jnp.concatenate([feats_rows(s, RIM, own_atoms).astype(F32) for s in range(samples)], axis=0)
    half[...] = (residual + mixed).astype(BF)
    span = 2 * width
    total = None
    for j in range(heads * token_cols // span):
        cols = slice(j * span, (j + 1) * span)
        pre = mm(half[...], w_tok[cols, :], NT)
        g1 = jax.nn.sigmoid(pre)
        acts[:, cols] = (pre * g1).astype(BF)
        ag = (spread[:, cols].astype(F32) * (g1 * (1.0 + pre * (1.0 - g1)))).astype(BF)
        ags[:, cols] = ag
        term = mm(ag, w_tok[cols, :])
        total = term if total is None else total + term
    mg[...] = total.astype(BF)
    og = mm(mg[...], w_out, NT)
    gt = gate[...]
    attg[...] = (gt * og).astype(BF)
    qg[:, width : 2 * width] = (og * att[...] * gt * (1.0 - gt)).astype(BF)
    for s, b in tiles:
        at = s * own_atoms + b * Q_WIN
        ma[s * blocks + b] = masked_stack(attg[at : at + Q_WIN, :].astype(F32))

    def head_blocks(a):
        return [a[h * depth : (h + 1) * depth, h * width : (h + 1) * width] for h in range(heads)]

    def head_scatter(buf, recv, sems):
        return [
            send(buf.at[lax.rem(me_h + k, heads)], recv.at[k - 1], sems, (k - 1,), head_peer(k)) for k in far_first
        ]

    def head_total(copies, buf, recv):
        value = buf[me_h].astype(F32)
        for copy in copies:
            copy.wait_recv()
        for k in range(1, heads):
            value = value + recv[k - 1].astype(F32)
        return value

    gtok = mm(ags[...], half[...], TN)
    gout = mm(hb[...], mg[...], TN)
    gvalue = head_blocks(mm(attg[...], zcat[...], TN))
    e_used = token_cols + 2 * depth
    for h in range(heads):
        eh[h, 0:token_cols, :] = gtok[h * token_cols : (h + 1) * token_cols].astype(BF)
        eh[h, token_cols : token_cols + depth, :] = gout[h * depth : (h + 1) * depth].astype(BF)
        eh[h, token_cols + depth : e_used, :] = gvalue[h].astype(BF)
        if e_used < eh.shape[1]:
            eh[h, e_used:, :] = jnp.zeros((eh.shape[1] - e_used, width), BF)
    eh_copies = head_scatter(eh, ehr, eh_sem)

    for s in range(samples):
        sums = mm(member, acts[s * own_atoms : (s + 1) * own_atoms, :])
        for h in range(heads):
            tsend[h, s * slots : (s + 1) * slots, :] = sums[:, h * token_cols : (h + 1) * token_cols].astype(BF)
    t_copies = head_scatter(tsend, trecv, t_sem)

    for s, b in tiles:
        t = s * blocks + b
        at = slice(s * own_atoms + b * Q_WIN, s * own_atoms + (b + 1) * Q_WIN)
        dp = mm(ma[t], window(s, b, 2, 3), NT)
        p = prob[t]
        ds = (p * (dp - jnp.sum(p * dp, axis=1, keepdims=True))).astype(BF)
        cols = slice(b * K_WIN, (b + 1) * K_WIN)
        if s == 0:
            dcat[:, cols] = ds
        else:
            dcat[:, cols] = (dcat[:, cols].astype(F32) + ds.astype(F32)).astype(BF)
        mixed_keys = mm(ds, window(s, b, 0, 2))
        qg[at, 0:width] = (scale * diagonal_pick(mixed_keys[:, 0:width])).astype(BF)
        for h in range(heads):
            ycat[at, h * width : (h + 1) * width] = mixed_keys[h * Q_WIN : (h + 1) * Q_WIN, width : 2 * width].astype(BF)

    def exchange_outer(value, where):
        if outer == 1:
            return value
        xbuf[where, 0, : value.shape[0], :] = value.astype(BF)
        copies = [
            send(xbuf.at[where, 0], xbuf.at[where, k], x_sem, (where, k - 1), outer_peer(k)) for k in range(1, outer)
        ]
        for k in range(1, outer):
            copies[k - 1].wait_recv()
            value = value + xbuf[where, k, : value.shape[0], :].astype(F32)
        return value

    def scatter(buf, recv, sems):
        return [
            send(buf.at[lax.rem(own + k, inner)], recv.at[k - 1], sems, (k - 1,), inner_peer(k))
            for k in range(1, inner)
        ]

    def total_of(copies, value, recv):
        for k in range(1, inner):
            copies[k - 1].wait_recv()
            value = value + recv[k - 1].astype(F32)
        return value

    def gather(res, value, sems):
        res[own] = value.astype(BF)
        return [send(res.at[own], res.at[own], sems, (k - 1,), inner_peer(k)) for k in range(1, inner)]

    def cut(buf, value):
        piece = buf.shape[1]
        value = value.astype(BF)
        for j in range(inner):
            buf[j] = value[j * piece : (j + 1) * piece]

    cut(ebuf, head_total(eh_copies, eh, ehr))
    e_copies = scatter(ebuf, erecv, e_sem)

    gqg = mm(qg[...], own_normed_again(keyed, samples, own_atoms, width), TN)
    gkey = head_blocks(mm(queries[...], ycat[...], TN))
    terms = jnp.where(diagonal, mm(dcat[...], pair[...], NT), 0.0)
    l_used = 4 * depth
    for h in range(heads):
        lh[h, 0:depth, :] = gqg[h * depth : (h + 1) * depth].astype(BF)
        lh[h, depth : 2 * depth, :] = gkey[h].astype(BF)
        lh[h, 2 * depth : 3 * depth, :] = gqg[(heads + h) * depth : (heads + h + 1) * depth].astype(BF)
        row = jnp.sum(terms[h * Q_WIN : (h + 1) * Q_WIN], axis=0, keepdims=True)
        folded = row[:, 0:width]
        for j in range(1, flat // width):
            folded = folded + row[:, j * width : (j + 1) * width]
        lh[h, 3 * depth :, :] = jnp.broadcast_to(folded, (lh.shape[1] - 3 * depth, width)).astype(BF)
    lh_copies = head_scatter(lh, lhr, lh_sem)

    tokens = head_total(t_copies, tsend, trecv)
    for s in range(samples):
        tok_out[s] = (tokens[s * slots : (s + 1) * slots] / divisor).astype(BF)

    total = exchange_outer(total_of(e_copies, ebuf[own].astype(F32), erecv), 0)
    eg_copies = gather(eres, total, eg_sem)
    cut(lbuf, head_total(lh_copies, lh, lhr))
    l_copies = scatter(lbuf, lrecv, l_sem)
    total = exchange_outer(total_of(l_copies, lbuf[own].astype(F32), lrecv), 1)
    lg_copies = gather(lres, total, lg_sem)

    def arrived(copies, res):
        for k in range(1, inner):
            copies[k - 1].wait_recv()
        return jnp.concatenate([res[j] for j in range(inner)], axis=0).astype(F32) * factor

    whole = arrived(eg_copies, eres)
    gtok_out[...] = whole[0:token_cols]
    gout_out[...] = whole[token_cols : token_cols + depth]
    gproj_out[2] = whole[token_cols + depth : e_used]
    whole = arrived(lg_copies, lres)
    gproj_out[0] = whole[0:depth]
    gproj_out[1] = whole[depth : 2 * depth]
    gproj_out[3] = whole[2 * depth : 3 * depth]
    pair_row = whole[3 * depth : 3 * depth + 1]
    channel_of = lax.rem(iota((channels, width), 1), channels) == iota((channels, width), 0)
    pair_col = jnp.sum(jnp.where(channel_of, pair_row, 0.0), axis=1, keepdims=True)
    across = iota((channels, width), 0) == iota((channels, width), 1)
    pair_row = jnp.sum(jnp.where(across, pair_col, 0.0), axis=0, keepdims=True)
    gpair_out[...] = pair_row[:, :channels]
    for copy in sends:
        copy.wait_send()


def own_normed_again(keyed, samples, own_atoms, width):
    return jnp.concatenate([keyed[s, RIM : RIM + own_atoms, width : 2 * width] for s in range(samples)], axis=0)


def on_device(atom_feats, pair_feats, tok_slot, w_proj, w_out, w_pair, w_tok, d_tok):
    samples, atoms, width = atom_feats.shape
    depth = w_proj.shape[2]
    slots, token_cols = d_tok.shape[1], d_tok.shape[2]
    channels = w_pair.shape[0]
    n = lax.axis_size("slab")
    heads = lax.axis_size("head")
    own_atoms = atoms // heads
    blocks = own_atoms // Q_WIN
    rows = samples * own_atoms
    tiles = samples * blocks
    stack = heads * Q_WIN
    flat = Q_WIN * channels
    reach = own_atoms + 2 * RIM
    tokens_w = heads * token_cols
    inner = next(m for m in (8, 4, 2, 1) if n % m == 0)
    outer = n // inner
    e_piece = -(-(token_cols + 2 * depth) // (16 * inner)) * 16
    l_piece = -(-(3 * depth + 1) // (16 * inner)) * 16
    peers = max(inner - 1, 1)
    far = max(outer - 1, 1)

    def vm(*shape, dtype=BF):
        return pltpu.VMEM(shape, dtype)

    def sems(*shape):
        return pltpu.SemaphoreType.DMA((2,) + shape)

    scratch = [
        vm(samples, atoms + 2 * RIM, width),
        vm(flat, blocks * K_WIN),
        vm(1, atoms, dtype=jnp.int32),
        vm(1, own_atoms, dtype=jnp.int32),
        vm(4, heads, depth, width),
        vm(heads, depth, width),
        vm(heads, 1, channels),
        vm(heads, token_cols, width),
        vm(heads, samples, slots, token_cols),
        vm(samples, reach, 3 * width),
        vm(stack, blocks * K_WIN, dtype=F32),
        vm(stack, flat),
        vm(rows, width),
        vm(rows, width, dtype=F32),
        vm(tiles, stack, width),
        vm(tiles, stack, K_WIN, dtype=F32),
        vm(rows, heads * width),
        vm(rows, width, dtype=F32),
        vm(rows, width),
        vm(rows, width),
        vm(samples, slots, tokens_w),
        vm(rows, tokens_w),
        vm(rows, tokens_w),
        vm(rows, tokens_w),
        vm(rows, width),
        vm(rows, width),
        vm(tiles, stack, width),
        vm(rows, 2 * width),
        vm(rows, heads * width),
        vm(stack, blocks * K_WIN),
        vm(heads, samples * slots, token_cols),
        vm(heads - 1, samples * slots, token_cols),
        vm(heads, inner * e_piece, width),
        vm(heads - 1, inner * e_piece, width),
        vm(inner, e_piece, width),
        vm(peers, e_piece, width),
        vm(inner, e_piece, width),
        vm(heads, inner * l_piece, width),
        vm(heads - 1, inner * l_piece, width),
        vm(inner, l_piece, width),
        vm(peers, l_piece, width),
        vm(inner, l_piece, width),
        vm(2, outer, max(e_piece, l_piece), width),
        pltpu.SemaphoreType.DMA((8,)),
        pltpu.SemaphoreType.DMA((blocks,)),
        sems(5, heads - 1),
        sems(2),
        sems(heads - 1),
        sems(heads - 1),
        sems(peers),
        sems(peers),
        sems(heads - 1),
        sems(peers),
        sems(peers),
        sems(2, far),
    ]
    in_vmem = pl.BlockSpec(memory_space=pltpu.VMEM)
    in_hbm = pl.BlockSpec(memory_space=pltpu.HBM)
    shapes = (
        jax.ShapeDtypeStruct((samples, slots, token_cols), BF),
        jax.ShapeDtypeStruct((4, depth, width), F32),
        jax.ShapeDtypeStruct((depth, width), F32),
        jax.ShapeDtypeStruct((1, channels), F32),
        jax.ShapeDtypeStruct((token_cols, width), F32),
    )
    results = pl.pallas_call(
        functools.partial(kernel, n, heads, inner),
        out_shape=shapes,
        in_specs=[in_hbm] * 8,
        out_specs=[in_vmem] * 5,
        scratch_shapes=scratch,
        compiler_params=pltpu.CompilerParams(
            collective_id=0, has_side_effects=True, vmem_limit_bytes=67043328
        ),
    )(
        atom_feats,
        pair_feats.reshape(atoms * channels, K_WIN),
        tok_slot.reshape(1, atoms),
        jnp.swapaxes(w_proj, 1, 2),
        w_out,
        w_pair.T,
        w_tok.T,
        d_tok,
    )
    tok_act, grad_proj, grad_out, grad_pair, grad_tok = pl.pallas_call(
        store,
        out_shape=shapes,
        in_specs=[in_vmem] * 5,
        out_specs=[in_hbm] * 5,
        scratch_shapes=[pltpu.SemaphoreType.DMA((5,))],
    )(*results)
    return tok_act, jnp.swapaxes(grad_proj, 1, 2), grad_out, grad_pair.T, grad_tok.T


def store(*refs):
    sem = refs[10]
    copies = [pltpu.make_async_copy(refs[i], refs[5 + i], sem.at[i]) for i in range(5)]
    for copy in copies:
        copy.start()
    for copy in copies:
        copy.wait()


def solution(mesh):
    return jax.shard_map(
        on_device,
        mesh=mesh,
        in_specs=(
            P(None, "slab", None),
            P("slab", None, None),
            P("slab"),
            P(None, None, "head"),
            P("head", None),
            P(None, "head"),
            P(None, "head"),
            P(None, "slab", "head"),
        ),
        out_specs=(
            P(None, "slab", "head"),
            P(None, None, "head"),
            P("head", None),
            P(None, "head"),
            P(None, "head"),
        ),
        check_vma=False,
    )
```

```python
import functools
import jax
import jax.numpy as jnp
from jax import lax
from jax.experimental import pallas as pl
from jax.experimental.pallas import tpu as pltpu
from jax.sharding import PartitionSpec as P

Q_WIN = 32
K_WIN = 128
RIM = 48
CORES = 2
GROUP = 8
EPSILON = 1e-05
MASKED = -1e30
BF = jnp.bfloat16
F32 = jnp.float32
NT = (((1,), (1,)), ((), ()))
NN = (((1,), (0,)), ((), ()))
TN = (((0,), (0,)), ((), ()))


def mm(a, b, dims=NN):
    return lax.dot_general(a, b, dims, preferred_element_type=F32)


def iota(shape, dim):
    return lax.broadcasted_iota(jnp.int32, shape, dim)


def layer_norm(x):
    x = x.astype(F32)
    centered = x - jnp.mean(x, axis=-1, keepdims=True)
    variance = jnp.mean(centered * centered, axis=-1, keepdims=True)
    return (centered * lax.rsqrt(variance + EPSILON)).astype(BF)


def kernel(
    n, heads, inner,
    feats_in, pair_in, slot_in, wproj_in, wout_in, wpair_in, wtok_in, dtok_in,
    tok_out, gproj_out, gout_out, gpair_out, gtok_out,
    fx, pair, slot, slot_own, wproj, wout, wpair, wtok, dtok,
    keyed, bias, mixer, queries, gate, prob, zcat, att, hcat, wcat, half, spread, acts, ags, mgs, mgr, mg, attg, qg, ycat, dcat,
    tsend, trecv, ebuf, erecv, eres, lbuf, lrecv, lres, xbuf,
    in_sem, pair_sem, w_sem, wo_sem, halo_sem, h_sem, m_sem, t_sem, e_sem, eg_sem, l_sem, lg_sem, x_sem,
):
    samples = fx.shape[0]
    width = fx.shape[2]
    atoms = fx.shape[1] - 2 * RIM
    chips, depth = wproj.shape[1], wproj.shape[2]
    side = chips * depth
    own_atoms = atoms // chips
    blocks = own_atoms // Q_WIN
    slots, token_cols = dtok.shape[2], dtok.shape[3]
    channels = wpair.shape[2]
    flat = Q_WIN * channels
    stack = chips * Q_WIN
    scale = depth ** (-0.5)
    factor = (samples * atoms * n) ** (-0.5)
    outer = n // inner
    me_s = lax.axis_index("slab")
    me_h = lax.axis_index("head")
    own = lax.rem(me_s, inner)
    base = me_s - own
    far_own = me_s // inner
    core = lax.rem(me_h, CORES)
    chip = me_h // CORES
    partner = {"head": me_h + 1 - 2 * core}
    sends = []

    def head_peer(k):
        return {"head": lax.rem(me_h + k, heads)}

    def chip_peer(d):
        return {"head": lax.rem(chip + d, chips) * CORES + core}

    def inner_peer(k):
        return {"slab": base + lax.rem(own + k, inner)}

    def block_peer(d, k):
        return {"slab": base + lax.rem(own + k, inner), "head": lax.rem(chip + d, chips) * CORES + core}

    def outer_peer(k):
        return {"slab": lax.rem(me_s + k * inner, n)}

    def ring_peer(k):
        return {"slab": lax.rem(me_s + k + n, n)}

    def send(src, dst, sems, index, device):
        copy = pltpu.make_async_remote_copy(
            src_ref=src, dst_ref=dst, send_sem=sems.at[(0,) + index], recv_sem=sems.at[(1,) + index],
            device_id=device, device_id_type=pl.DeviceIdType.MESH,
        )
        copy.start()
        sends.append(copy)
        return copy

    def arrive(copies):
        for copy in copies:
            copy.wait_recv()

    greeted = [head_peer(k) for k in range(1, heads)] + [inner_peer(k) for k in range(1, inner)]
    greeted += [block_peer(d, k) for d in range(1, chips) for k in range(1, inner)]
    greeted += [outer_peer(k) for k in range(1, outer)]
    if outer > 1:
        greeted += [ring_peer(1), ring_peer(-1)]
    barrier = pltpu.get_barrier_semaphore()
    for device in greeted:
        pl.semaphore_signal(barrier, inc=1, device_id=device, device_id_type=pl.DeviceIdType.MESH)

    first_atom = pl.multiple_of(chip * own_atoms, own_atoms)
    loads = [
        pltpu.make_async_copy(a, b, in_sem.at[i])
        for i, (a, b) in enumerate(
            [
                (feats_in, fx.at[:, RIM : RIM + atoms, :]),
                (wproj_in, wproj.at[:, chip]),
                (wout_in, wout.at[core, chip]),
                (slot_in, slot),
                (slot_in.at[:, pl.ds(first_atom, own_atoms)], slot_own),
                (dtok_in, dtok.at[chip]),
                (wpair_in, wpair.at[chip]),
                (wtok_in, wtok.at[chip]),
            ]
        )
    ]
    pair_loads = [
        pltpu.make_async_copy(
            pair_in.at[pl.ds(pl.multiple_of(first_atom * channels, flat) + b * flat, flat), :],
            pair.at[:, b * K_WIN : (b + 1) * K_WIN],
            pair_sem.at[b],
        )
        for b in range(blocks)
    ]
    for load in loads + pair_loads:
        load.start()

    pl.semaphore_wait(barrier, len(greeted))

    def share_far(i, src, dst):
        return [send(src, dst, w_sem, (i, d - 1), chip_peer(d)) for d in range(1, chips)]

    wproj_copies = share_far(0, wproj_in, wproj.at[:, chip])
    wpair_copies = share_far(1, wpair_in, wpair.at[chip])
    to_left = send(
        feats_in.at[:, 0:RIM, :], fx.at[:, RIM + atoms : RIM + atoms + RIM, :], halo_sem, (1,), ring_peer(-1)
    )
    to_right = send(feats_in.at[:, atoms - RIM : atoms, :], fx.at[:, 0:RIM, :], halo_sem, (0,), ring_peer(1))
    wout_copies = [send(wout_in, wout.at[core, chip], wo_sem, (k - 1,), head_peer(k)) for k in range(1, heads)]
    wtok_copies = share_far(2, wtok_in, wtok.at[chip])
    dtok_copies = share_far(3, dtok_in, dtok.at[chip])

    lane_group = iota((Q_WIN, width), 1) // depth

    def masked_stack(wide, first):
        wide = wide.astype(F32)
        parts = [jnp.where(lane_group == first + h, wide, 0.0) for h in range(chips)]
        return jnp.concatenate(parts, axis=0).astype(BF)

    def diagonal_pick(tall):
        out = tall[0:Q_WIN]
        for h in range(1, chips):
            out = jnp.where(lax.rem(lane_group, chips) == h, tall[h * Q_WIN : (h + 1) * Q_WIN], out)
        return out

    def feats_rows(s, start, size):
        return fx[s, pl.ds(first_atom + start, size), :]

    def sample(s):
        return slice(s * own_atoms, (s + 1) * own_atoms)

    loads[0].wait()
    for s in range(samples):
        keyed[s, RIM : RIM + own_atoms, width : 2 * width] = layer_norm(feats_rows(s, RIM, own_atoms))

    loads[3].wait()
    loads[4].wait()
    slot_ids = me_s * slots
    member = jnp.where(slot[...] == slot_ids + iota((slots, atoms), 0), 1.0, 0.0)
    divisor = jnp.maximum(jnp.sum(member, axis=1, keepdims=True), 1.0)
    member = jnp.where(slot_own[...] == slot_ids + iota((slots, own_atoms), 0), 1.0, 0.0).astype(BF)

    loads[1].wait()
    arrive(wproj_copies)
    query_gate = jnp.concatenate([wproj[0].reshape(side, width), wproj[3].reshape(side, width)], axis=0)
    key_value = wproj[1:3].reshape(2 * side, width)
    for s in range(samples):
        projected = mm(keyed[s, RIM : RIM + own_atoms, width : 2 * width], query_gate, NT)
        queries[sample(s), :] = (projected * scale).astype(BF)
        gate[sample(s), :] = jax.nn.sigmoid(projected)

    to_right.wait_recv()
    to_left.wait_recv()
    for s in range(samples):
        for start in (0, RIM + own_atoms):
            keyed[s, start : start + RIM, width : 2 * width] = layer_norm(feats_rows(s, start, RIM))
        keyed[s, :, 0:width] = mm(keyed[s, :, width : 2 * width], key_value, NT).astype(BF)

    loads[6].wait()
    arrive(wpair_copies)
    picker = lax.rem(iota((channels, flat), 1), channels) == iota((channels, flat), 0)
    w_tall = jnp.concatenate(
        [jnp.broadcast_to(wpair[h].astype(F32), (Q_WIN, channels)) for h in range(chips)], axis=0
    ).astype(BF)
    w_rows = mm(w_tall, picker.astype(F32).astype(BF))
    diagonal = iota((stack, flat), 1) // channels == lax.rem(iota((stack, flat), 0), Q_WIN)
    mixer[...] = jnp.where(diagonal, w_rows, 0.0).astype(BF)
    for load in pair_loads:
        load.wait()
    block_start = (me_s * chips + chip) * own_atoms - RIM
    reach = K_WIN - Q_WIN - RIM
    for b in range(blocks):
        cols = slice(b * K_WIN, (b + 1) * K_WIN)
        bias[:, cols] = mm(mixer[...], pair[:, cols])
        if b * Q_WIN < RIM or (b + 1) * Q_WIN + reach > own_atoms:
            where = block_start + b * Q_WIN + iota((stack, K_WIN), 1)
            bias[:, cols] = jnp.where((where >= 0) & (where < atoms * n), bias[:, cols], MASKED)

    def tile(s, b):
        return slice(s * own_atoms + b * Q_WIN, s * own_atoms + (b + 1) * Q_WIN)

    def window(s, b, wide):
        return keyed[s, b * Q_WIN : b * Q_WIN + K_WIN, 0 : wide * width]

    def forward(s, group):
        raw = [
            mm(masked_stack(queries[tile(s, b), :], 0), window(s, b, 1), NT) + bias[:, b * K_WIN : (b + 1) * K_WIN]
            for b in group
        ]
        tops = [jnp.max(scores, axis=1, keepdims=True) for scores in raw]
        powers = [jnp.exp(scores - top) for scores, top in zip(raw, tops)]
        sums = [jnp.sum(e, axis=1, keepdims=True) for e in powers]
        weights = [e * (1.0 / total) for e, total in zip(powers, sums)]
        for b, p in zip(group, weights):
            prob[s * blocks + b] = p
        results = [mm(p.astype(BF), window(s, b, 2)) for b, p in zip(group, weights)]
        for b, mixed_values in zip(group, results):
            at = tile(s, b)
            for h in range(chips):
                part = mixed_values[h * Q_WIN : (h + 1) * Q_WIN, width : 2 * width]
                zcat[at, h * width : (h + 1) * width] = part.astype(BF)
            attended = diagonal_pick(mixed_values[:, 0:width])
            att[at, :] = attended
            hcat[at, 0:width] = (gate[at, :] * attended).astype(BF)

    groups = [range(b, min(b + GROUP, blocks)) for b in range(0, blocks, GROUP)]

    h_copies = []
    for s in range(samples):
        for group in groups:
            forward(s, group)
        h_copies.append(send(hcat.at[sample(s), 0:width], hcat.at[sample(s), width : 2 * width], h_sem, (s,), partner))

    loads[2].wait()
    arrive(wout_copies)
    blank = jnp.zeros((side, width), BF)
    wcat[0:side, :] = blank
    wcat[side : 2 * side, :] = wout[core].reshape(side, width)
    wcat[2 * side : 3 * side, :] = blank
    wcat[3 * side : 4 * side, :] = wout[1 - core].reshape(side, width)
    loads[7].wait()
    arrive(wtok_copies)
    w_tok = wtok.reshape(chips * token_cols, width)
    loads[5].wait()
    arrive(dtok_copies)
    for s in range(samples):
        wide = jnp.concatenate([dtok[h, s].astype(F32) for h in range(chips)], axis=1)
        spread[sample(s), :] = mm(member, (wide / divisor).astype(BF), TN).astype(BF)

    m_copies = []
    span = 2 * width
    columns = chips * token_cols
    for s in range(samples):
        at = sample(s)
        h_copies[s].wait_recv()
        mixed = feats_rows(s, RIM, own_atoms).astype(F32) + mm(hcat[at, :], wcat[...])
        half[at, :] = mixed.astype(BF)
        total = None
        for start in range(0, columns, span):
            cols = slice(start, min(start + span, columns))
            pre = mm(half[at, :], w_tok[cols, :], NT)
            g1 = jax.nn.sigmoid(pre)
            acts[at, cols] = (pre * g1).astype(BF)
            ag = (spread[at, cols].astype(F32) * (g1 * (1.0 + pre * (1.0 - g1)))).astype(BF)
            ags[at, cols] = ag
            term = mm(ag, w_tok[cols, :])
            total = term if total is None else total + term
        mgs[at, :] = total.astype(BF)
        m_copies.append(send(mgs.at[at], mgr.at[at], m_sem, (s,), partner))

    gtok = mm(ags[...], half[...], TN)

    def before_backward(s):
        at = sample(s)
        m_copies[s].wait_recv()
        total = (mgs[at, :].astype(F32) + mgr[at, :].astype(F32)).astype(BF)
        mg[at, :] = total
        og = mm(total, wcat[0 : 2 * side, :], NT)
        gt = gate[at, :]
        attg[at, :] = (gt * og).astype(BF)
        qg[at, :] = (og * att[at, :] * gt * (1.0 - gt)).astype(BF)

    def backward(s, group):
        slopes = [mm(masked_stack(attg[tile(s, b), :], chips), window(s, b, 1), NT) for b in group]
        probs = [prob[s * blocks + b] for b in group]
        sums = [jnp.sum(p * dp, axis=1, keepdims=True) for p, dp in zip(probs, slopes)]
        grads = [(p * (dp - total)).astype(BF) for p, dp, total in zip(probs, slopes, sums)]
        results = [mm(ds, window(s, b, 2)) for b, ds in zip(group, grads)]
        for b, ds in zip(group, grads):
            cols = slice(b * K_WIN, (b + 1) * K_WIN)
            if s == 0:
                dcat[:, cols] = ds
            else:
                dcat[:, cols] = (dcat[:, cols].astype(F32) + ds.astype(F32)).astype(BF)
        for b, mixed_keys in zip(group, results):
            at = tile(s, b)
            query_grad = scale * diagonal_pick(mixed_keys[:, 0:width])
            qg[at, :] = jnp.where(lane_group < chips, query_grad, qg[at, :].astype(F32)).astype(BF)
            for h in range(chips):
                part = mixed_keys[h * Q_WIN : (h + 1) * Q_WIN, width : 2 * width]
                ycat[at, h * width : (h + 1) * width] = part.astype(BF)

    def head_block(a, h, first):
        return a[first + h * depth : first + (h + 1) * depth, h * width : (h + 1) * width]

    offsets = [(d, k) for d in range(chips) for k in range(inner) if d or k]

    def pack(buf, h, parts):
        piece = buf.shape[2]
        spare = inner * piece - sum(part.shape[0] for part in parts)
        if spare:
            parts = parts + [jnp.zeros((spare, width), F32)]
        packed = jnp.concatenate(parts, axis=0).astype(BF)
        for j in range(inner):
            buf[h, j] = packed[j * piece : (j + 1) * piece]

    def scatter(buf, recv, sems):
        return [
            send(buf.at[lax.rem(chip + d, chips), lax.rem(own + k, inner)], recv.at[i], sems, (i,), block_peer(d, k))
            for i, (d, k) in enumerate(offsets)
        ]

    def total_of(copies, buf, recv):
        total = buf[chip, own].astype(F32)
        for i, copy in enumerate(copies):
            copy.wait_recv()
            total = total + recv[i].astype(F32)
        return total

    def exchange_outer(value, where):
        if outer == 1:
            return value
        part = xbuf.at[where, far_own, pl.ds(0, value.shape[0])]
        part[...] = value.astype(BF)
        copies = [send(part, part, x_sem, (where, k - 1), outer_peer(k)) for k in range(1, outer)]
        for copy in copies:
            copy.wait_recv()
        value = xbuf[where, 0, 0 : value.shape[0], :].astype(F32)
        for k in range(1, outer):
            value = value + xbuf[where, k, 0 : value.shape[0], :].astype(F32)
        return value

    def gather(res, value, sems):
        res[own] = value.astype(BF)
        return [send(res.at[own], res.at[own], sems, (k - 1,), inner_peer(k)) for k in range(1, inner)]

    def gathered(copies, res):
        arrive(copies)
        return jnp.concatenate([res[j] for j in range(inner)], axis=0).astype(F32) * factor

    for s in range(samples):
        before_backward(s)
        if s == samples - 1:
            gout = mm(hcat[:, 0:width], mg[...], TN)
            gvalue = mm(attg[...], zcat[...], TN)
            for h in range(chips):
                tail = [gout[side + h * depth : side + (h + 1) * depth], head_block(gvalue, h, side)]
                pack(ebuf, h, [gtok[h * token_cols : (h + 1) * token_cols]] + tail)
            e_copies = scatter(ebuf, erecv, e_sem)
        for group in groups:
            backward(s, group)

    normed = jnp.concatenate([keyed[s, RIM : RIM + own_atoms, width : 2 * width] for s in range(samples)], axis=0)
    gqg = mm(qg[...], normed, TN)
    gkey = mm(queries[...], ycat[...], TN)
    terms = jnp.where(diagonal, mm(dcat[...], pair[...], NT), 0.0)
    for h in range(chips):
        row = jnp.sum(terms[h * Q_WIN : (h + 1) * Q_WIN], axis=0, keepdims=True)
        folded = row[:, 0:width]
        for j in range(1, flat // width):
            folded = folded + row[:, j * width : (j + 1) * width]
        gates = gqg[side + h * depth : side + (h + 1) * depth]
        lines = [gqg[h * depth : (h + 1) * depth], head_block(gkey, h, 0), gates, jnp.broadcast_to(folded, (8, width))]
        pack(lbuf, h, lines)
    l_copies = scatter(lbuf, lrecv, l_sem)

    for s in range(samples):
        sums = mm(member, acts[sample(s), :])
        for h in range(chips):
            tsend[h, s * slots : (s + 1) * slots, :] = sums[:, h * token_cols : (h + 1) * token_cols].astype(BF)
    t_copies = [
        send(tsend.at[lax.rem(chip + d, chips)], trecv.at[d - 1], t_sem, (d - 1,), chip_peer(d)) for d in range(1, chips)
    ]

    eg_copies = gather(eres, exchange_outer(total_of(e_copies, ebuf, erecv), 0), eg_sem)
    lg_copies = gather(lres, exchange_outer(total_of(l_copies, lbuf, lrecv), 1), lg_sem)
    tokens = tsend[chip].astype(F32)
    for d in range(1, chips):
        t_copies[d - 1].wait_recv()
        tokens = tokens + trecv[d - 1].astype(F32)
    for s in range(samples):
        tok_out[s] = (tokens[s * slots : (s + 1) * slots] / divisor).astype(BF)

    whole = gathered(eg_copies, eres)
    gtok_out[...] = whole[0:token_cols]
    gout_out[...] = whole[token_cols : token_cols + depth]
    gproj_out[2] = whole[token_cols + depth : token_cols + 2 * depth]
    whole = gathered(lg_copies, lres)
    gproj_out[0] = whole[0:depth]
    gproj_out[1] = whole[depth : 2 * depth]
    gproj_out[3] = whole[2 * depth : 3 * depth]
    pair_row = whole[3 * depth : 3 * depth + 1]
    channel_of = lax.rem(iota((channels, width), 1), channels) == iota((channels, width), 0)
    pair_col = jnp.sum(jnp.where(channel_of, pair_row, 0.0), axis=1, keepdims=True)
    across = iota((channels, width), 0) == iota((channels, width), 1)
    pair_row = jnp.sum(jnp.where(across, pair_col, 0.0), axis=0, keepdims=True)
    gpair_out[...] = pair_row[:, :channels]
    for copy in sends:
        copy.wait_send()


def on_device(atom_feats, pair_feats, tok_slot, w_proj, w_out, w_pair, w_tok, d_tok):
    samples, atoms, width = atom_feats.shape
    depth = w_proj.shape[2]
    slots, token_cols = d_tok.shape[1], d_tok.shape[2]
    channels = w_pair.shape[0]
    n = lax.axis_size("slab")
    heads = lax.axis_size("head")
    chips = heads // CORES
    own_atoms = atoms // chips
    blocks = own_atoms // Q_WIN
    rows = samples * own_atoms
    stack = chips * Q_WIN
    flat = Q_WIN * channels
    columns = chips * token_cols
    inner = next(m for m in (8, 4, 2, 1) if n % m == 0)
    outer = n // inner
    e_piece = -(-(token_cols + 2 * depth) // (16 * inner)) * 16
    l_piece = -(-(3 * depth + 8) // (16 * inner)) * 16
    peers = max(inner - 1, 1)
    far = max(outer - 1, 1)
    others = max(chips * inner - 1, 1)

    def vm(*shape, dtype=BF):
        return pltpu.VMEM(shape, dtype)

    def sems(*shape):
        return pltpu.SemaphoreType.DMA((2,) + shape)

    scratch = [
        vm(samples, atoms + 2 * RIM, width),
        vm(flat, blocks * K_WIN),
        vm(1, atoms, dtype=jnp.int32),
        vm(1, own_atoms, dtype=jnp.int32),
        vm(4, chips, depth, width),
        vm(CORES, chips, depth, width),
        vm(chips, 1, channels),
        vm(chips, token_cols, width),
        vm(chips, samples, slots, token_cols),
        vm(samples, own_atoms + 2 * RIM, 2 * width),
        vm(stack, blocks * K_WIN, dtype=F32),
        vm(stack, flat),
        vm(rows, width),
        vm(rows, width, dtype=F32),
        vm(samples * blocks, stack, K_WIN, dtype=F32),
        vm(rows, chips * width),
        vm(rows, width, dtype=F32),
        vm(rows, 2 * width),
        vm(2 * width, width),
        vm(rows, width),
        vm(rows, columns),
        vm(rows, columns),
        vm(rows, columns),
        vm(rows, width),
        vm(rows, width),
        vm(rows, width),
        vm(rows, width),
        vm(rows, width),
        vm(rows, chips * width),
        vm(stack, blocks * K_WIN),
        vm(chips, samples * slots, token_cols),
        vm(max(chips - 1, 1), samples * slots, token_cols),
        vm(chips, inner, e_piece, width),
        vm(others, e_piece, width),
        vm(inner, e_piece, width),
        vm(chips, inner, l_piece, width),
        vm(others, l_piece, width),
        vm(inner, l_piece, width),
        vm(2, outer, max(e_piece, l_piece), width),
        pltpu.SemaphoreType.DMA((8,)),
        pltpu.SemaphoreType.DMA((blocks,)),
        sems(4, max(chips - 1, 1)),
        sems(heads - 1),
        sems(2),
        sems(samples),
        sems(samples),
        sems(max(chips - 1, 1)),
        sems(others),
        sems(peers),
        sems(others),
        sems(peers),
        sems(2, far),
    ]
    in_vmem = pl.BlockSpec(memory_space=pltpu.VMEM)
    in_hbm = pl.BlockSpec(memory_space=pltpu.HBM)
    shapes = (
        jax.ShapeDtypeStruct((samples, slots, token_cols), BF),
        jax.ShapeDtypeStruct((4, depth, width), F32),
        jax.ShapeDtypeStruct((depth, width), F32),
        jax.ShapeDtypeStruct((1, channels), F32),
        jax.ShapeDtypeStruct((token_cols, width), F32),
    )
    results = pl.pallas_call(
        functools.partial(kernel, n, heads, inner),
        out_shape=shapes,
        in_specs=[in_hbm] * 8,
        out_specs=[in_vmem] * 5,
        scratch_shapes=scratch,
        compiler_params=pltpu.CompilerParams(
            collective_id=0, has_side_effects=True, vmem_limit_bytes=67043328
        ),
    )(
        atom_feats,
        pair_feats.reshape(atoms * channels, K_WIN),
        tok_slot.reshape(1, atoms),
        jnp.swapaxes(w_proj, 1, 2),
        w_out,
        w_pair.T,
        w_tok.T,
        d_tok,
    )
    tok_act, grad_proj, grad_out, grad_pair, grad_tok = pl.pallas_call(
        store,
        out_shape=shapes,
        in_specs=[in_vmem] * 5,
        out_specs=[in_hbm] * 5,
        scratch_shapes=[pltpu.SemaphoreType.DMA((5,))],
    )(*results)
    return tok_act, jnp.swapaxes(grad_proj, 1, 2), grad_out, grad_pair.T, grad_tok.T


def store(*refs):
    sem = refs[10]
    copies = [pltpu.make_async_copy(refs[i], refs[5 + i], sem.at[i]) for i in range(5)]
    for copy in copies:
        copy.start()
    for copy in copies:
        copy.wait()


def solution(mesh):
    return jax.shard_map(
        on_device,
        mesh=mesh,
        in_specs=(
            P(None, "slab", None),
            P("slab", None, None),
            P("slab"),
            P(None, None, "head"),
            P("head", None),
            P(None, "head"),
            P(None, "head"),
            P(None, "slab", "head"),
        ),
        out_specs=(
            P(None, "slab", "head"),
            P(None, None, "head"),
            P("head", None),
            P(None, "head"),
            P(None, "head"),
        ),
        check_vma=False,
    )
```

```python
import functools
import jax
import jax.numpy as jnp
from jax import lax
from jax.experimental import pallas as pl
from jax.experimental.pallas import tpu as pltpu
from jax.sharding import PartitionSpec as P

Q_WIN = 32
K_WIN = 128
RIM = 48
CORES = 2
GROUP = 8
EPSILON = 1e-05
MASKED = -1e30
BF = jnp.bfloat16
F32 = jnp.float32
NT = (((1,), (1,)), ((), ()))
NN = (((1,), (0,)), ((), ()))
TN = (((0,), (0,)), ((), ()))


def mm(a, b, dims=NN):
    return lax.dot_general(a, b, dims, preferred_element_type=F32)


def iota(shape, dim):
    return lax.broadcasted_iota(jnp.int32, shape, dim)


def layer_norm(x):
    x = x.astype(F32)
    centered = x - jnp.mean(x, axis=-1, keepdims=True)
    variance = jnp.mean(centered * centered, axis=-1, keepdims=True)
    return (centered * lax.rsqrt(variance + EPSILON)).astype(BF)


def kernel(
    n, heads, inner,
    feats_in, pair_in, slot_in, wproj_in, wout_in, wpair_in, wtok_in, dtok_in,
    tok_out, gproj_out, gout_out, gpair_out, gtok_out,
    fx, pair, slot, slot_own, wproj, wout, wpair, wtok, dtok,
    keyed, bias, mixer, queries, gate, prob, zcat, att, hcat, wcat, half, spread, acts, ags, mgs, mgr, mg, attg, qg, ycat, dcat,
    tsend, trecv, ebuf, erecv, eres, lbuf, lrecv, lres, xbuf,
    in_sem, pair_sem, w_sem, wo_sem, halo_sem, h_sem, m_sem, t_sem, e_sem, eg_sem, l_sem, lg_sem, x_sem,
):
    samples = fx.shape[0]
    width = fx.shape[2]
    atoms = fx.shape[1] - 2 * RIM
    chips, depth = wproj.shape[1], wproj.shape[2]
    side = chips * depth
    own_atoms = atoms // chips
    blocks = own_atoms // Q_WIN
    slots, token_cols = dtok.shape[2], dtok.shape[3]
    channels = wpair.shape[2]
    flat = Q_WIN * channels
    stack = chips * Q_WIN
    scale = depth ** (-0.5)
    factor = (samples * atoms * n) ** (-0.5)
    outer = n // inner
    me_s = lax.axis_index("slab")
    me_h = lax.axis_index("head")
    own = lax.rem(me_s, inner)
    base = me_s - own
    far_own = me_s // inner
    core = lax.rem(me_h, CORES)
    chip = me_h // CORES
    partner = {"head": me_h + 1 - 2 * core}
    reducers = ebuf.shape[1]
    first_reducer = (inner - reducers) // 2
    sends = []
    guarded = []

    def head_peer(k):
        return {"head": lax.rem(me_h + k, heads)}

    def chip_peer(d):
        return {"head": lax.rem(chip + d, chips) * CORES + core}

    def inner_peer(k):
        return {"slab": base + lax.rem(own + k, inner)}

    def block_peer(d, k):
        return {"slab": base + lax.rem(own + k, inner), "head": lax.rem(chip + d, chips) * CORES + core}

    def outer_peer(k):
        return {"slab": lax.rem(me_s + k * inner, n)}

    def ring_peer(k):
        return {"slab": lax.rem(me_s + k + n, n)}

    def send(src, dst, sems, index, device):
        copy = pltpu.make_async_remote_copy(
            src_ref=src, dst_ref=dst, send_sem=sems.at[(0,) + index], recv_sem=sems.at[(1,) + index],
            device_id=device, device_id_type=pl.DeviceIdType.MESH,
        )
        copy.start()
        sends.append(copy)
        return copy

    def arrive(copies):
        for copy in copies:
            copy.wait_recv()

    greeted = [head_peer(k) for k in range(1, heads)] + [inner_peer(k) for k in range(1, inner)]
    greeted += [block_peer(d, k) for d in range(1, chips) for k in range(1, inner)]
    greeted += [outer_peer(k) for k in range(1, outer)]
    if outer > 1:
        greeted += [ring_peer(1), ring_peer(-1)]
    barrier = pltpu.get_barrier_semaphore()
    for device in greeted:
        pl.semaphore_signal(barrier, inc=1, device_id=device, device_id_type=pl.DeviceIdType.MESH)

    first_atom = pl.multiple_of(chip * own_atoms, own_atoms)
    loads = [
        pltpu.make_async_copy(a, b, in_sem.at[i])
        for i, (a, b) in enumerate(
            [
                (feats_in, fx.at[:, RIM : RIM + atoms, :]),
                (wproj_in, wproj.at[:, chip]),
                (wout_in, wout.at[core, chip]),
                (slot_in, slot),
                (slot_in.at[:, pl.ds(first_atom, own_atoms)], slot_own),
                (dtok_in, dtok.at[chip]),
                (wpair_in, wpair.at[chip]),
                (wtok_in, wtok.at[chip]),
            ]
        )
    ]
    pair_loads = [
        pltpu.make_async_copy(
            pair_in.at[pl.ds(pl.multiple_of(first_atom * channels, flat) + b * flat, flat), :],
            pair.at[:, b * K_WIN : (b + 1) * K_WIN],
            pair_sem.at[b],
        )
        for b in range(blocks)
    ]
    for load in loads + pair_loads:
        load.start()

    pl.semaphore_wait(barrier, len(greeted))

    def share_far(i, src, dst):
        return [send(src, dst, w_sem, (i, d - 1), chip_peer(d)) for d in range(1, chips)]

    wpair_copies = share_far(1, wpair_in, wpair.at[chip])
    wproj_copies = share_far(0, wproj_in, wproj.at[:, chip])
    to_left = send(
        feats_in.at[:, 0:RIM, :], fx.at[:, RIM + atoms : RIM + atoms + RIM, :], halo_sem, (1,), ring_peer(-1)
    )
    to_right = send(feats_in.at[:, atoms - RIM : atoms, :], fx.at[:, 0:RIM, :], halo_sem, (0,), ring_peer(1))
    wout_copies = [send(wout_in, wout.at[core, chip], wo_sem, (k - 1,), head_peer(k)) for k in range(1, heads)]
    wtok_copies = share_far(2, wtok_in, wtok.at[chip])
    dtok_copies = share_far(3, dtok_in, dtok.at[chip])

    lane_group = iota((Q_WIN, width), 1) // depth

    def masked_stack(wide, first):
        wide = wide.astype(F32)
        parts = [jnp.where(lane_group == first + h, wide, 0.0) for h in range(chips)]
        return jnp.concatenate(parts, axis=0).astype(BF)

    def diagonal_pick(tall):
        out = tall[0:Q_WIN]
        for h in range(1, chips):
            out = jnp.where(lax.rem(lane_group, chips) == h, tall[h * Q_WIN : (h + 1) * Q_WIN], out)
        return out

    def feats_rows(s, start, size):
        return fx[s, pl.ds(first_atom + start, size), :]

    def sample(s):
        return slice(s * own_atoms, (s + 1) * own_atoms)

    loads[0].wait()
    for s in range(samples):
        keyed[s, RIM : RIM + own_atoms, width : 2 * width] = layer_norm(feats_rows(s, RIM, own_atoms))

    loads[3].wait()
    loads[4].wait()
    slot_ids = me_s * slots
    member = jnp.where(slot[...] == slot_ids + iota((slots, atoms), 0), 1.0, 0.0)
    divisor = jnp.maximum(jnp.sum(member, axis=1, keepdims=True), 1.0)
    member = jnp.where(slot_own[...] == slot_ids + iota((slots, own_atoms), 0), 1.0, 0.0).astype(BF)

    loads[6].wait()
    arrive(wpair_copies)
    picker = lax.rem(iota((channels, flat), 1), channels) == iota((channels, flat), 0)
    w_tall = jnp.concatenate(
        [jnp.broadcast_to(wpair[h].astype(F32), (Q_WIN, channels)) for h in range(chips)], axis=0
    ).astype(BF)
    w_rows = mm(w_tall, picker.astype(F32).astype(BF))
    diagonal = iota((stack, flat), 1) // channels == lax.rem(iota((stack, flat), 0), Q_WIN)
    mixer[...] = jnp.where(diagonal, w_rows, 0.0).astype(BF)
    for load in pair_loads:
        load.wait()
    block_start = (me_s * chips + chip) * own_atoms - RIM
    reach = K_WIN - Q_WIN - RIM
    for b in range(blocks):
        cols = slice(b * K_WIN, (b + 1) * K_WIN)
        bias[:, cols] = mm(mixer[...], pair[:, cols])
        if b * Q_WIN < RIM or (b + 1) * Q_WIN + reach > own_atoms:
            where = block_start + b * Q_WIN + iota((stack, K_WIN), 1)
            bias[:, cols] = jnp.where((where >= 0) & (where < atoms * n), bias[:, cols], MASKED)

    loads[1].wait()
    arrive(wproj_copies)
    query_gate = jnp.concatenate([wproj[0].reshape(side, width), wproj[3].reshape(side, width)], axis=0)
    key_value = wproj[1:3].reshape(2 * side, width)
    for s in range(samples):
        projected = mm(keyed[s, RIM : RIM + own_atoms, width : 2 * width], query_gate, NT)
        queries[sample(s), :] = (projected * scale).astype(BF)
        gate[sample(s), :] = jax.nn.sigmoid(projected)

    to_right.wait_recv()
    to_left.wait_recv()
    for s in range(samples):
        for start in (0, RIM + own_atoms):
            keyed[s, start : start + RIM, width : 2 * width] = layer_norm(feats_rows(s, start, RIM))
        keyed[s, :, 0:width] = mm(keyed[s, :, width : 2 * width], key_value, NT).astype(BF)

    def tile(s, b):
        return slice(s * own_atoms + b * Q_WIN, s * own_atoms + (b + 1) * Q_WIN)

    def window(s, b, wide):
        return keyed[s, b * Q_WIN : b * Q_WIN + K_WIN, 0 : wide * width]

    def forward(s, group):
        raw = [
            mm(masked_stack(queries[tile(s, b), :], 0), window(s, b, 1), NT) + bias[:, b * K_WIN : (b + 1) * K_WIN]
            for b in group
        ]
        tops = [jnp.max(scores, axis=1, keepdims=True) for scores in raw]
        powers = [jnp.exp(scores - top) for scores, top in zip(raw, tops)]
        sums = [jnp.sum(e, axis=1, keepdims=True) for e in powers]
        weights = [e * (1.0 / total) for e, total in zip(powers, sums)]
        for b, p in zip(group, weights):
            prob[s * blocks + b] = p
        results = [mm(p.astype(BF), window(s, b, 2)) for b, p in zip(group, weights)]
        for b, mixed_values in zip(group, results):
            at = tile(s, b)
            for h in range(chips):
                part = mixed_values[h * Q_WIN : (h + 1) * Q_WIN, width : 2 * width]
                zcat[at, h * width : (h + 1) * width] = part.astype(BF)
            attended = diagonal_pick(mixed_values[:, 0:width])
            att[at, :] = attended
            hcat[at, 0:width] = (gate[at, :] * attended).astype(BF)

    groups = [range(b, min(b + GROUP, blocks)) for b in range(0, blocks, GROUP)]

    h_copies = []
    for s in range(samples):
        for group in groups:
            forward(s, group)
        h_copies.append(send(hcat.at[sample(s), 0:width], hcat.at[sample(s), width : 2 * width], h_sem, (s,), partner))

    loads[2].wait()
    arrive(wout_copies)
    blank = jnp.zeros((side, width), BF)
    wcat[0:side, :] = blank
    wcat[side : 2 * side, :] = wout[core].reshape(side, width)
    wcat[2 * side : 3 * side, :] = blank
    wcat[3 * side : 4 * side, :] = wout[1 - core].reshape(side, width)
    loads[7].wait()
    arrive(wtok_copies)
    w_tok = wtok.reshape(chips * token_cols, width)
    loads[5].wait()
    arrive(dtok_copies)
    for s in range(samples):
        wide = jnp.concatenate([dtok[h, s].astype(F32) for h in range(chips)], axis=1)
        spread[sample(s), :] = mm(member, (wide / divisor).astype(BF), TN).astype(BF)

    m_copies = []
    span = 2 * width
    columns = chips * token_cols
    for s in range(samples):
        at = sample(s)
        h_copies[s].wait_recv()
        mixed = feats_rows(s, RIM, own_atoms).astype(F32) + mm(hcat[at, :], wcat[...])
        half[at, :] = mixed.astype(BF)
        total = None
        for start in range(0, columns, span):
            cols = slice(start, min(start + span, columns))
            pre = mm(half[at, :], w_tok[cols, :], NT)
            g1 = jax.nn.sigmoid(pre)
            acts[at, cols] = (pre * g1).astype(BF)
            ag = (spread[at, cols].astype(F32) * (g1 * (1.0 + pre * (1.0 - g1)))).astype(BF)
            ags[at, cols] = ag
            term = mm(ag, w_tok[cols, :])
            total = term if total is None else total + term
        mgs[at, :] = total.astype(BF)
        m_copies.append(send(mgs.at[at], mgr.at[at], m_sem, (s,), partner))

    gtok = mm(ags[...], half[...], TN)

    def before_backward(s):
        at = sample(s)
        m_copies[s].wait_recv()
        total = (mgs[at, :].astype(F32) + mgr[at, :].astype(F32)).astype(BF)
        mg[at, :] = total
        og = mm(total, wcat[0 : 2 * side, :], NT)
        gt = gate[at, :]
        attg[at, :] = (gt * og).astype(BF)
        qg[at, :] = (og * att[at, :] * gt * (1.0 - gt)).astype(BF)

    def backward(s, group):
        slopes = [mm(masked_stack(attg[tile(s, b), :], chips), window(s, b, 1), NT) for b in group]
        probs = [prob[s * blocks + b] for b in group]
        sums = [jnp.sum(p * dp, axis=1, keepdims=True) for p, dp in zip(probs, slopes)]
        grads = [(p * (dp - total)).astype(BF) for p, dp, total in zip(probs, slopes, sums)]
        results = [mm(ds, window(s, b, 2)) for b, ds in zip(group, grads)]
        for b, ds in zip(group, grads):
            cols = slice(b * K_WIN, (b + 1) * K_WIN)
            if s == 0:
                dcat[:, cols] = ds
            else:
                dcat[:, cols] = (dcat[:, cols].astype(F32) + ds.astype(F32)).astype(BF)
        for b, mixed_keys in zip(group, results):
            at = tile(s, b)
            query_grad = scale * diagonal_pick(mixed_keys[:, 0:width])
            qg[at, :] = jnp.where(lane_group < chips, query_grad, qg[at, :].astype(F32)).astype(BF)
            for h in range(chips):
                part = mixed_keys[h * Q_WIN : (h + 1) * Q_WIN, width : 2 * width]
                ycat[at, h * width : (h + 1) * width] = part.astype(BF)

    def head_block(a, h, first):
        return a[first + h * depth : first + (h + 1) * depth, h * width : (h + 1) * width]

    def pack(buf, h, parts):
        piece = buf.shape[2]
        spare = reducers * piece - sum(part.shape[0] for part in parts)
        if spare:
            parts = parts + [jnp.zeros((spare, width), F32)]
        packed = jnp.concatenate(parts, axis=0).astype(BF)
        for j in range(reducers):
            buf[h, j] = packed[j * piece : (j + 1) * piece]

    def scatter(buf, recv, sems):
        for d in range(chips):
            for r in range(reducers):
                copy = pltpu.make_async_remote_copy(
                    src_ref=buf.at[lax.rem(chip + d, chips), r], dst_ref=recv.at[d, own],
                    send_sem=sems.at[0, d, r], recv_sem=sems.at[1, d, own],
                    device_id={"slab": base + first_reducer + r, "head": lax.rem(chip + d, chips) * CORES + core},
                    device_id_type=pl.DeviceIdType.MESH,
                )
                if d:
                    copy.start()
                    sends.append(copy)
                else:
                    pl.when(own != first_reducer + r)(copy.start)
                    guarded.append((own != first_reducer + r, copy))

    def reduce(buf, recv, sems, res, res_sems, where):
        mine = own - first_reducer

        @pl.when((own >= first_reducer) & (own < first_reducer + reducers))
        def _():
            recv[0, own] = buf[chip, mine]
            for d in range(chips):
                for i in range(inner):
                    copy = pltpu.make_async_remote_copy(
                        src_ref=buf.at[0, 0], dst_ref=recv.at[d, i], send_sem=sems.at[0, d, 0], recv_sem=sems.at[1, d, i],
                        device_id=inner_peer(1), device_id_type=pl.DeviceIdType.MESH,
                    )
                    if d:
                        copy.wait_recv()
                    else:
                        pl.when(own != i)(copy.wait_recv)
            total = None
            for d in range(chips):
                for i in range(inner):
                    term = recv[d, i].astype(F32)
                    total = term if total is None else total + term
            res[mine] = exchange_outer(total, where).astype(BF)
            for k in range(1, inner):
                share(res, res_sems, k).start()

    def share(res, res_sems, k):
        mine = own - first_reducer
        return pltpu.make_async_remote_copy(
            src_ref=res.at[mine], dst_ref=res.at[mine], send_sem=res_sems.at[0, k - 1], recv_sem=res_sems.at[1, mine],
            device_id=inner_peer(k), device_id_type=pl.DeviceIdType.MESH,
        )

    def exchange_outer(value, where):
        if outer == 1:
            return value
        part = xbuf.at[where, far_own, pl.ds(0, value.shape[0])]
        part[...] = value.astype(BF)
        copies = [
            pltpu.make_async_remote_copy(
                src_ref=part, dst_ref=part, send_sem=x_sem.at[0, where, k - 1], recv_sem=x_sem.at[1, where, k - 1],
                device_id=outer_peer(k), device_id_type=pl.DeviceIdType.MESH,
            )
            for k in range(1, outer)
        ]
        for copy in copies:
            copy.start()
        for copy in copies:
            copy.wait()
        value = xbuf[where, 0, 0 : value.shape[0], :].astype(F32)
        for k in range(1, outer):
            value = value + xbuf[where, k, 0 : value.shape[0], :].astype(F32)
        return value

    def gathered(res, res_sems):
        for r in range(reducers):
            copy = pltpu.make_async_remote_copy(
                src_ref=res.at[r], dst_ref=res.at[r], send_sem=res_sems.at[0, 0], recv_sem=res_sems.at[1, r],
                device_id=inner_peer(1), device_id_type=pl.DeviceIdType.MESH,
            )
            pl.when(own != first_reducer + r)(copy.wait_recv)
        return jnp.concatenate([res[r] for r in range(reducers)], axis=0).astype(F32) * factor

    for s in range(samples):
        before_backward(s)
        if s == samples - 1:
            gout = mm(hcat[:, 0:width], mg[...], TN)
            gvalue = mm(attg[...], zcat[...], TN)
            for h in range(chips):
                tail = [gout[side + h * depth : side + (h + 1) * depth], head_block(gvalue, h, side)]
                pack(ebuf, h, [gtok[h * token_cols : (h + 1) * token_cols]] + tail)
            scatter(ebuf, erecv, e_sem)
        for group in groups:
            backward(s, group)

    normed = jnp.concatenate([keyed[s, RIM : RIM + own_atoms, width : 2 * width] for s in range(samples)], axis=0)
    gqg = mm(qg[...], normed, TN)
    gkey = mm(queries[...], ycat[...], TN)
    terms = jnp.where(diagonal, mm(dcat[...], pair[...], NT), 0.0)
    for h in range(chips):
        row = jnp.sum(terms[h * Q_WIN : (h + 1) * Q_WIN], axis=0, keepdims=True)
        folded = row[:, 0:width]
        for j in range(1, flat // width):
            folded = folded + row[:, j * width : (j + 1) * width]
        gates = gqg[side + h * depth : side + (h + 1) * depth]
        lines = [gqg[h * depth : (h + 1) * depth], head_block(gkey, h, 0), gates, jnp.broadcast_to(folded, (8, width))]
        pack(lbuf, h, lines)
    scatter(lbuf, lrecv, l_sem)

    for s in range(samples):
        sums = mm(member, acts[sample(s), :])
        for h in range(chips):
            tsend[h, s * slots : (s + 1) * slots, :] = sums[:, h * token_cols : (h + 1) * token_cols].astype(BF)
    t_copies = [
        send(tsend.at[lax.rem(chip + d, chips)], trecv.at[d - 1], t_sem, (d - 1,), chip_peer(d)) for d in range(1, chips)
    ]

    reduce(ebuf, erecv, e_sem, eres, eg_sem, 0)
    reduce(lbuf, lrecv, l_sem, lres, lg_sem, 1)
    tokens = tsend[chip].astype(F32)
    for d in range(1, chips):
        t_copies[d - 1].wait_recv()
        tokens = tokens + trecv[d - 1].astype(F32)
    for s in range(samples):
        tok_out[s] = (tokens[s * slots : (s + 1) * slots] / divisor).astype(BF)

    whole = gathered(eres, eg_sem)
    gtok_out[...] = whole[0:token_cols]
    gout_out[...] = whole[token_cols : token_cols + depth]
    gproj_out[2] = whole[token_cols + depth : token_cols + 2 * depth]
    whole = gathered(lres, lg_sem)
    gproj_out[0] = whole[0:depth]
    gproj_out[1] = whole[depth : 2 * depth]
    gproj_out[3] = whole[2 * depth : 3 * depth]
    pair_row = whole[3 * depth : 3 * depth + 1]
    channel_of = lax.rem(iota((channels, width), 1), channels) == iota((channels, width), 0)
    pair_col = jnp.sum(jnp.where(channel_of, pair_row, 0.0), axis=1, keepdims=True)
    across = iota((channels, width), 0) == iota((channels, width), 1)
    pair_row = jnp.sum(jnp.where(across, pair_col, 0.0), axis=0, keepdims=True)
    gpair_out[...] = pair_row[:, :channels]
    for copy in sends:
        copy.wait_send()
    for unlike, copy in guarded:
        pl.when(unlike)(copy.wait_send)

    @pl.when((own >= first_reducer) & (own < first_reducer + reducers))
    def _():
        for k in range(1, inner):
            share(eres, eg_sem, k).wait_send()
            share(lres, lg_sem, k).wait_send()


def on_device(atom_feats, pair_feats, tok_slot, w_proj, w_out, w_pair, w_tok, d_tok):
    samples, atoms, width = atom_feats.shape
    depth = w_proj.shape[2]
    slots, token_cols = d_tok.shape[1], d_tok.shape[2]
    channels = w_pair.shape[0]
    n = lax.axis_size("slab")
    heads = lax.axis_size("head")
    chips = heads // CORES
    own_atoms = atoms // chips
    blocks = own_atoms // Q_WIN
    rows = samples * own_atoms
    stack = chips * Q_WIN
    flat = Q_WIN * channels
    columns = chips * token_cols
    inner = next(m for m in (8, 4, 2, 1) if n % m == 0)
    outer = n // inner
    reducers = inner // 2 if inner > 2 else inner
    e_piece = -(-(token_cols + 2 * depth) // (16 * reducers)) * 16
    l_piece = -(-(3 * depth + 8) // (16 * reducers)) * 16
    far = max(outer - 1, 1)

    def vm(*shape, dtype=BF):
        return pltpu.VMEM(shape, dtype)

    def sems(*shape):
        return pltpu.SemaphoreType.DMA((2,) + shape)

    scratch = [
        vm(samples, atoms + 2 * RIM, width),
        vm(flat, blocks * K_WIN),
        vm(1, atoms, dtype=jnp.int32),
        vm(1, own_atoms, dtype=jnp.int32),
        vm(4, chips, depth, width),
        vm(CORES, chips, depth, width),
        vm(chips, 1, channels),
        vm(chips, token_cols, width),
        vm(chips, samples, slots, token_cols),
        vm(samples, own_atoms + 2 * RIM, 2 * width),
        vm(stack, blocks * K_WIN, dtype=F32),
        vm(stack, flat),
        vm(rows, width),
        vm(rows, width, dtype=F32),
        vm(samples * blocks, stack, K_WIN, dtype=F32),
        vm(rows, chips * width),
        vm(rows, width, dtype=F32),
        vm(rows, 2 * width),
        vm(2 * width, width),
        vm(rows, width),
        vm(rows, columns),
        vm(rows, columns),
        vm(rows, columns),
        vm(rows, width),
        vm(rows, width),
        vm(rows, width),
        vm(rows, width),
        vm(rows, width),
        vm(rows, chips * width),
        vm(stack, blocks * K_WIN),
        vm(chips, samples * slots, token_cols),
        vm(max(chips - 1, 1), samples * slots, token_cols),
        vm(chips, reducers, e_piece, width),
        vm(chips, inner, e_piece, width),
        vm(reducers, e_piece, width),
        vm(chips, reducers, l_piece, width),
        vm(chips, inner, l_piece, width),
        vm(reducers, l_piece, width),
        vm(2, outer, max(e_piece, l_piece), width),
        pltpu.SemaphoreType.DMA((8,)),
        pltpu.SemaphoreType.DMA((blocks,)),
        sems(4, max(chips - 1, 1)),
        sems(heads - 1),
        sems(2),
        sems(samples),
        sems(samples),
        sems(max(chips - 1, 1)),
        sems(chips, inner),
        sems(inner),
        sems(chips, inner),
        sems(inner),
        sems(2, far),
    ]
    in_vmem = pl.BlockSpec(memory_space=pltpu.VMEM)
    in_hbm = pl.BlockSpec(memory_space=pltpu.HBM)
    shapes = (
        jax.ShapeDtypeStruct((samples, slots, token_cols), BF),
        jax.ShapeDtypeStruct((4, depth, width), F32),
        jax.ShapeDtypeStruct((depth, width), F32),
        jax.ShapeDtypeStruct((1, channels), F32),
        jax.ShapeDtypeStruct((token_cols, width), F32),
    )
    results = pl.pallas_call(
        functools.partial(kernel, n, heads, inner),
        out_shape=shapes,
        in_specs=[in_hbm] * 8,
        out_specs=[in_vmem] * 5,
        scratch_shapes=scratch,
        compiler_params=pltpu.CompilerParams(
            collective_id=0, has_side_effects=True, vmem_limit_bytes=67043328
        ),
    )(
        atom_feats,
        pair_feats.reshape(atoms * channels, K_WIN),
        tok_slot.reshape(1, atoms),
        jnp.swapaxes(w_proj, 1, 2),
        w_out,
        w_pair.T,
        w_tok.T,
        d_tok,
    )
    tok_act, grad_proj, grad_out, grad_pair, grad_tok = pl.pallas_call(
        store,
        out_shape=shapes,
        in_specs=[in_vmem] * 5,
        out_specs=[in_hbm] * 5,
        scratch_shapes=[pltpu.SemaphoreType.DMA((5,))],
    )(*results)
    return tok_act, jnp.swapaxes(grad_proj, 1, 2), grad_out, grad_pair.T, grad_tok.T


def store(*refs):
    sem = refs[10]
    copies = [pltpu.make_async_copy(refs[i], refs[5 + i], sem.at[i]) for i in range(5)]
    for copy in copies:
        copy.start()
    for copy in copies:
        copy.wait()


def solution(mesh):
    return jax.shard_map(
        on_device,
        mesh=mesh,
        in_specs=(
            P(None, "slab", None),
            P("slab", None, None),
            P("slab"),
            P(None, None, "head"),
            P("head", None),
            P(None, "head"),
            P(None, "head"),
            P(None, "slab", "head"),
        ),
        out_specs=(
            P(None, "slab", "head"),
            P(None, None, "head"),
            P("head", None),
            P(None, "head"),
            P(None, "head"),
        ),
        check_vma=False,
    )
```

```python
import functools
import jax
import jax.numpy as jnp
from jax import lax
from jax.experimental import pallas as pl
from jax.experimental.pallas import tpu as pltpu
from jax.sharding import PartitionSpec as P

Q_WIN = 32
K_WIN = 128
RIM = 48
CORES = 2
GROUP = 8
EPSILON = 1e-05
MASKED = -1e30
BF = jnp.bfloat16
F32 = jnp.float32
NT = (((1,), (1,)), ((), ()))
NN = (((1,), (0,)), ((), ()))
TN = (((0,), (0,)), ((), ()))


def mm(a, b, dims=NN):
    return lax.dot_general(a, b, dims, preferred_element_type=F32)


def iota(shape, dim):
    return lax.broadcasted_iota(jnp.int32, shape, dim)


def layer_norm(x):
    x = x.astype(F32)
    centered = x - jnp.mean(x, axis=-1, keepdims=True)
    variance = jnp.mean(centered * centered, axis=-1, keepdims=True)
    return (centered * lax.rsqrt(variance + EPSILON)).astype(BF)


def kernel(
    n, heads, inner,
    feats_in, pair_in, slot_in, wproj_in, wout_in, wpair_in, wtok_in, dtok_in,
    tok_out, gproj_out, gout_out, gpair_out, gtok_out,
    fx, pair, slot, slot_own, wproj, wout, wpair, wtok, dtok,
    keyed, bias, mixer, queries, gate, prob, zcat, att, hcat, wcat, half, spread, acts, ags, mgs, mgr, mg, attg, qg, ycat, dcat,
    tsend, trecv, ebuf, erecv, eres, lbuf, lrecv, lres, xbuf,
    in_sem, pair_sem, w_sem, wo_sem, halo_sem, h_sem, m_sem, t_sem, e_sem, eg_sem, l_sem, lg_sem, x_sem,
):
    samples = fx.shape[0]
    width = fx.shape[2]
    atoms = fx.shape[1] - 2 * RIM
    chips, depth = wproj.shape[1], wproj.shape[2]
    side = chips * depth
    own_atoms = atoms // chips
    blocks = own_atoms // Q_WIN
    slots, token_cols = dtok.shape[2], dtok.shape[3]
    channels = wpair.shape[2]
    flat = Q_WIN * channels
    stack = chips * Q_WIN
    scale = depth ** (-0.5)
    factor = (samples * atoms * n) ** (-0.5)
    outer = n // inner
    me_s = lax.axis_index("slab")
    me_h = lax.axis_index("head")
    own = lax.rem(me_s, inner)
    base = me_s - own
    far_own = me_s // inner
    core = lax.rem(me_h, CORES)
    chip = me_h // CORES
    partner = {"head": me_h + 1 - 2 * core}
    reducers = ebuf.shape[1]
    first_reducer = (inner - reducers) // 2
    sends = []
    guarded = []

    def head_peer(k):
        return {"head": lax.rem(me_h + k, heads)}

    def chip_peer(d):
        return {"head": lax.rem(chip + d, chips) * CORES + core}

    def inner_peer(k):
        return {"slab": base + lax.rem(own + k, inner)}

    def block_peer(d, k):
        return {"slab": base + lax.rem(own + k, inner), "head": lax.rem(chip + d, chips) * CORES + core}

    def outer_peer(k):
        return {"slab": lax.rem(me_s + k * inner, n)}

    def ring_peer(k):
        return {"slab": lax.rem(me_s + k + n, n)}

    def send(src, dst, sems, index, device):
        copy = pltpu.make_async_remote_copy(
            src_ref=src, dst_ref=dst, send_sem=sems.at[(0,) + index], recv_sem=sems.at[(1,) + index],
            device_id=device, device_id_type=pl.DeviceIdType.MESH,
        )
        copy.start()
        sends.append(copy)
        return copy

    def arrive(copies):
        for copy in copies:
            copy.wait_recv()

    greeted = [head_peer(k) for k in range(1, heads)] + [inner_peer(k) for k in range(1, inner)]
    greeted += [block_peer(d, k) for d in range(1, chips) for k in range(1, inner)]
    greeted += [outer_peer(k) for k in range(1, outer)]
    if outer > 1:
        greeted += [ring_peer(1), ring_peer(-1)]
    barrier = pltpu.get_barrier_semaphore()
    for device in greeted:
        pl.semaphore_signal(barrier, inc=1, device_id=device, device_id_type=pl.DeviceIdType.MESH)

    first_atom = pl.multiple_of(chip * own_atoms, own_atoms)
    loads = [
        pltpu.make_async_copy(a, b, in_sem.at[i])
        for i, (a, b) in enumerate(
            [
                (feats_in, fx.at[:, RIM : RIM + atoms, :]),
                (wproj_in, wproj.at[:, chip]),
                (wout_in, wout.at[core, chip]),
                (slot_in, slot),
                (slot_in.at[:, pl.ds(first_atom, own_atoms)], slot_own),
                (dtok_in, dtok.at[chip]),
                (wpair_in, wpair.at[chip]),
                (wtok_in, wtok.at[chip]),
            ]
        )
    ]
    pair_loads = [
        pltpu.make_async_copy(
            pair_in.at[pl.ds(pl.multiple_of(first_atom * channels, flat) + b * flat, flat), :],
            pair.at[:, b * K_WIN : (b + 1) * K_WIN],
            pair_sem.at[b],
        )
        for b in range(blocks)
    ]
    for load in loads + pair_loads:
        load.start()

    pl.semaphore_wait(barrier, len(greeted))

    def share_far(i, src, dst):
        return [send(src, dst, w_sem, (i, d - 1), chip_peer(d)) for d in range(1, chips)]

    wpair_copies = share_far(1, wpair_in, wpair.at[chip])
    wproj_copies = share_far(0, wproj_in, wproj.at[:, chip])
    to_left = send(
        feats_in.at[:, 0:RIM, :], fx.at[:, RIM + atoms : RIM + atoms + RIM, :], halo_sem, (1,), ring_peer(-1)
    )
    to_right = send(feats_in.at[:, atoms - RIM : atoms, :], fx.at[:, 0:RIM, :], halo_sem, (0,), ring_peer(1))
    wout_copies = [send(wout_in, wout.at[core, chip], wo_sem, (k - 1,), head_peer(k)) for k in range(1, heads)]
    wtok_copies = share_far(2, wtok_in, wtok.at[chip])
    dtok_copies = share_far(3, dtok_in, dtok.at[chip])

    lane_group = iota((Q_WIN, width), 1) // depth

    def masked_stack(wide, first):
        wide = wide.astype(F32)
        parts = [jnp.where(lane_group == first + h, wide, 0.0) for h in range(chips)]
        return jnp.concatenate(parts, axis=0).astype(BF)

    def diagonal_pick(tall):
        out = tall[0:Q_WIN]
        for h in range(1, chips):
            out = jnp.where(lax.rem(lane_group, chips) == h, tall[h * Q_WIN : (h + 1) * Q_WIN], out)
        return out

    def feats_rows(s, start, size):
        return fx[s, pl.ds(first_atom + start, size), :]

    def sample(s):
        return slice(s * own_atoms, (s + 1) * own_atoms)

    loads[0].wait()
    for s in range(samples):
        keyed[s, RIM : RIM + own_atoms, width : 2 * width] = layer_norm(feats_rows(s, RIM, own_atoms))

    loads[3].wait()
    loads[4].wait()
    slot_ids = me_s * slots
    member = jnp.where(slot[...] == slot_ids + iota((slots, atoms), 0), 1.0, 0.0)
    divisor = jnp.maximum(jnp.sum(member, axis=1, keepdims=True), 1.0)
    member = jnp.where(slot_own[...] == slot_ids + iota((slots, own_atoms), 0), 1.0, 0.0).astype(BF)

    loads[6].wait()
    arrive(wpair_copies)
    picker = lax.rem(iota((channels, flat), 1), channels) == iota((channels, flat), 0)
    w_tall = jnp.concatenate(
        [jnp.broadcast_to(wpair[h].astype(F32), (Q_WIN, channels)) for h in range(chips)], axis=0
    ).astype(BF)
    w_rows = mm(w_tall, picker.astype(F32).astype(BF))
    diagonal = iota((stack, flat), 1) // channels == lax.rem(iota((stack, flat), 0), Q_WIN)
    mixer[...] = jnp.where(diagonal, w_rows, 0.0).astype(BF)
    for load in pair_loads:
        load.wait()
    block_start = (me_s * chips + chip) * own_atoms - RIM
    reach = K_WIN - Q_WIN - RIM
    for b in range(blocks):
        cols = slice(b * K_WIN, (b + 1) * K_WIN)
        bias[:, cols] = mm(mixer[...], pair[:, cols])
        if b * Q_WIN < RIM or (b + 1) * Q_WIN + reach > own_atoms:
            where = block_start + b * Q_WIN + iota((stack, K_WIN), 1)
            bias[:, cols] = jnp.where((where >= 0) & (where < atoms * n), bias[:, cols], MASKED)

    loads[1].wait()
    arrive(wproj_copies)
    query_gate = jnp.concatenate([wproj[0].reshape(side, width), wproj[3].reshape(side, width)], axis=0)
    key_value = wproj[1:3].reshape(2 * side, width)
    def project(s):
        projected = mm(keyed[s, RIM : RIM + own_atoms, width : 2 * width], query_gate, NT)
        queries[sample(s), :] = (projected * scale).astype(BF)
        gate[sample(s), :] = jax.nn.sigmoid(projected)

        for start in (0, RIM + own_atoms):
            keyed[s, start : start + RIM, width : 2 * width] = layer_norm(feats_rows(s, start, RIM))
        keyed[s, :, 0:width] = mm(keyed[s, :, width : 2 * width], key_value, NT).astype(BF)

    to_right.wait_recv()
    to_left.wait_recv()
    def tile(s, b):
        return slice(s * own_atoms + b * Q_WIN, s * own_atoms + (b + 1) * Q_WIN)

    def window(s, b, wide):
        return keyed[s, b * Q_WIN : b * Q_WIN + K_WIN, 0 : wide * width]

    def forward(s, group):
        raw = [
            mm(masked_stack(queries[tile(s, b), :], 0), window(s, b, 1), NT) + bias[:, b * K_WIN : (b + 1) * K_WIN]
            for b in group
        ]
        tops = [jnp.max(scores, axis=1, keepdims=True) for scores in raw]
        powers = [jnp.exp(scores - top) for scores, top in zip(raw, tops)]
        sums = [jnp.sum(e, axis=1, keepdims=True) for e in powers]
        weights = [e * (1.0 / total) for e, total in zip(powers, sums)]
        for b, p in zip(group, weights):
            prob[s * blocks + b] = p
        results = [mm(p.astype(BF), window(s, b, 2)) for b, p in zip(group, weights)]
        for b, mixed_values in zip(group, results):
            at = tile(s, b)
            for h in range(chips):
                part = mixed_values[h * Q_WIN : (h + 1) * Q_WIN, width : 2 * width]
                zcat[at, h * width : (h + 1) * width] = part.astype(BF)
            attended = diagonal_pick(mixed_values[:, 0:width])
            att[at, :] = attended
            hcat[at, 0:width] = (gate[at, :] * attended).astype(BF)

    groups = [range(b, min(b + GROUP, blocks)) for b in range(0, blocks, GROUP)]

    h_copies = []
    for s in range(samples):
        project(s)
        for group in groups:
            forward(s, group)
        h_copies.append(send(hcat.at[sample(s), 0:width], hcat.at[sample(s), width : 2 * width], h_sem, (s,), partner))

    loads[2].wait()
    arrive(wout_copies)
    blank = jnp.zeros((side, width), BF)
    wcat[0:side, :] = blank
    wcat[side : 2 * side, :] = wout[core].reshape(side, width)
    wcat[2 * side : 3 * side, :] = blank
    wcat[3 * side : 4 * side, :] = wout[1 - core].reshape(side, width)
    loads[7].wait()
    arrive(wtok_copies)
    w_tok = wtok.reshape(chips * token_cols, width)
    loads[5].wait()
    arrive(dtok_copies)
    def spread_tokens(s):
        wide = jnp.concatenate([dtok[h, s].astype(F32) for h in range(chips)], axis=1)
        spread[sample(s), :] = mm(member, (wide / divisor).astype(BF), TN).astype(BF)

    m_copies = []
    span = 2 * width
    columns = chips * token_cols
    def middle(s):
        at = sample(s)
        h_copies[s].wait_recv()
        mixed = feats_rows(s, RIM, own_atoms).astype(F32) + mm(hcat[at, :], wcat[...])
        half[at, :] = mixed.astype(BF)
        total = None
        for start in range(0, columns, span):
            cols = slice(start, min(start + span, columns))
            pre = mm(half[at, :], w_tok[cols, :], NT)
            g1 = jax.nn.sigmoid(pre)
            acts[at, cols] = (pre * g1).astype(BF)
            ag = (spread[at, cols].astype(F32) * (g1 * (1.0 + pre * (1.0 - g1)))).astype(BF)
            ags[at, cols] = ag
            term = mm(ag, w_tok[cols, :])
            total = term if total is None else total + term
        mgs[at, :] = total.astype(BF)
        m_copies.append(send(mgs.at[at], mgr.at[at], m_sem, (s,), partner))

    def token_sums(s):
        sums = mm(member, acts[sample(s), :])
        for h in range(chips):
            tsend[h, s * slots : (s + 1) * slots, :] = sums[:, h * token_cols : (h + 1) * token_cols].astype(BF)


    def before_backward(s):
        at = sample(s)
        m_copies[s].wait_recv()
        total = (mgs[at, :].astype(F32) + mgr[at, :].astype(F32)).astype(BF)
        mg[at, :] = total
        og = mm(total, wcat[0 : 2 * side, :], NT)
        gt = gate[at, :]
        attg[at, :] = (gt * og).astype(BF)
        qg[at, :] = (og * att[at, :] * gt * (1.0 - gt)).astype(BF)

    def backward(s, group):
        slopes = [mm(masked_stack(attg[tile(s, b), :], chips), window(s, b, 1), NT) for b in group]
        probs = [prob[s * blocks + b] for b in group]
        sums = [jnp.sum(p * dp, axis=1, keepdims=True) for p, dp in zip(probs, slopes)]
        grads = [(p * (dp - total)).astype(BF) for p, dp, total in zip(probs, slopes, sums)]
        results = [mm(ds, window(s, b, 2)) for b, ds in zip(group, grads)]
        for b, ds in zip(group, grads):
            cols = slice(b * K_WIN, (b + 1) * K_WIN)
            if s == 0:
                dcat[:, cols] = ds
            else:
                dcat[:, cols] = (dcat[:, cols].astype(F32) + ds.astype(F32)).astype(BF)
        for b, mixed_keys in zip(group, results):
            at = tile(s, b)
            query_grad = scale * diagonal_pick(mixed_keys[:, 0:width])
            qg[at, :] = jnp.where(lane_group < chips, query_grad, qg[at, :].astype(F32)).astype(BF)
            for h in range(chips):
                part = mixed_keys[h * Q_WIN : (h + 1) * Q_WIN, width : 2 * width]
                ycat[at, h * width : (h + 1) * width] = part.astype(BF)

    def head_block(a, h, first):
        return a[first + h * depth : first + (h + 1) * depth, h * width : (h + 1) * width]

    def pack(buf, h, parts):
        piece = buf.shape[2]
        spare = reducers * piece - sum(part.shape[0] for part in parts)
        if spare:
            parts = parts + [jnp.zeros((spare, width), F32)]
        packed = jnp.concatenate(parts, axis=0).astype(BF)
        for j in range(reducers):
            buf[h, j] = packed[j * piece : (j + 1) * piece]

    def scatter(buf, recv, sems):
        for d in range(chips):
            for r in range(reducers):
                copy = pltpu.make_async_remote_copy(
                    src_ref=buf.at[lax.rem(chip + d, chips), r], dst_ref=recv.at[d, own],
                    send_sem=sems.at[0, d, r], recv_sem=sems.at[1, d, own],
                    device_id={"slab": base + first_reducer + r, "head": lax.rem(chip + d, chips) * CORES + core},
                    device_id_type=pl.DeviceIdType.MESH,
                )
                if d:
                    copy.start()
                    sends.append(copy)
                else:
                    pl.when(own != first_reducer + r)(copy.start)
                    guarded.append((own != first_reducer + r, copy))

    def reduce(buf, recv, sems, res, res_sems, where):
        mine = own - first_reducer

        @pl.when((own >= first_reducer) & (own < first_reducer + reducers))
        def _():
            recv[0, own] = buf[chip, mine]
            for d in range(chips):
                for i in range(inner):
                    copy = pltpu.make_async_remote_copy(
                        src_ref=buf.at[0, 0], dst_ref=recv.at[d, i], send_sem=sems.at[0, d, 0], recv_sem=sems.at[1, d, i],
                        device_id=inner_peer(1), device_id_type=pl.DeviceIdType.MESH,
                    )
                    if d:
                        copy.wait_recv()
                    else:
                        pl.when(own != i)(copy.wait_recv)
            total = None
            for d in range(chips):
                for i in range(inner):
                    term = recv[d, i].astype(F32)
                    total = term if total is None else total + term
            res[mine] = exchange_outer(total, where).astype(BF)
            for k in range(1, inner):
                share(res, res_sems, k).start()

    def share(res, res_sems, k):
        mine = own - first_reducer
        return pltpu.make_async_remote_copy(
            src_ref=res.at[mine], dst_ref=res.at[mine], send_sem=res_sems.at[0, k - 1], recv_sem=res_sems.at[1, mine],
            device_id=inner_peer(k), device_id_type=pl.DeviceIdType.MESH,
        )

    def exchange_outer(value, where):
        if outer == 1:
            return value
        part = xbuf.at[where, far_own, pl.ds(0, value.shape[0])]
        part[...] = value.astype(BF)
        copies = [
            pltpu.make_async_remote_copy(
                src_ref=part, dst_ref=part, send_sem=x_sem.at[0, where, k - 1], recv_sem=x_sem.at[1, where, k - 1],
                device_id=outer_peer(k), device_id_type=pl.DeviceIdType.MESH,
            )
            for k in range(1, outer)
        ]
        for copy in copies:
            copy.start()
        for copy in copies:
            copy.wait()
        value = xbuf[where, 0, 0 : value.shape[0], :].astype(F32)
        for k in range(1, outer):
            value = value + xbuf[where, k, 0 : value.shape[0], :].astype(F32)
        return value

    def shared(res, res_sems):
        @pl.when((own >= first_reducer) & (own < first_reducer + reducers))
        def _():
            for k in range(1, inner):
                share(res, res_sems, k).wait_send()

    def gathered(res, res_sems):
        for r in range(reducers):
            copy = pltpu.make_async_remote_copy(
                src_ref=res.at[r], dst_ref=res.at[r], send_sem=res_sems.at[0, 0], recv_sem=res_sems.at[1, r],
                device_id=inner_peer(1), device_id_type=pl.DeviceIdType.MESH,
            )
            pl.when(own != first_reducer + r)(copy.wait_recv)
        return jnp.concatenate([res[r] for r in range(reducers)], axis=0).astype(F32) * factor

    gtok = None
    for s in range(samples):
        spread_tokens(s)
        middle(s)
        term = mm(ags[sample(s), :], half[sample(s), :], TN)
        gtok = term if gtok is None else gtok + term
        if s < samples - 1:
            token_sums(s)
    for h in range(chips):
        pack(ebuf, h, [gtok[h * token_cols : (h + 1) * token_cols]])
    scatter(ebuf, erecv, e_sem)
    token_sums(samples - 1)
    t_copies = [
        send(tsend.at[lax.rem(chip + d, chips)], trecv.at[d - 1], t_sem, (d - 1,), chip_peer(d)) for d in range(1, chips)
    ]

    for s in range(samples):
        before_backward(s)
        if s == samples - 1:
            gout = mm(hcat[:, 0:width], mg[...], TN)
            gvalue = mm(attg[...], zcat[...], TN)
        for group in groups:
            backward(s, group)
        normed = keyed[s, RIM : RIM + own_atoms, width : 2 * width]
        terms = (mm(qg[sample(s), :], normed, TN), mm(queries[sample(s), :], ycat[sample(s), :], TN))
        late = terms if s == 0 else [before + term for before, term in zip(late, terms)]

    gqg, gkey = late
    terms = jnp.where(diagonal, mm(dcat[...], pair[...], NT), 0.0)
    for h in range(chips):
        row = jnp.sum(terms[h * Q_WIN : (h + 1) * Q_WIN], axis=0, keepdims=True)
        folded = row[:, 0:width]
        for j in range(1, flat // width):
            folded = folded + row[:, j * width : (j + 1) * width]
        gates = gqg[side + h * depth : side + (h + 1) * depth]
        lines = [gqg[h * depth : (h + 1) * depth], head_block(gkey, h, 0), gates, head_block(gvalue, h, side)]
        lines += [gout[side + h * depth : side + (h + 1) * depth], jnp.broadcast_to(folded, (8, width))]
        pack(lbuf, h, lines)
    scatter(lbuf, lrecv, l_sem)

    reduce(ebuf, erecv, e_sem, eres, eg_sem, 0)
    reduce(lbuf, lrecv, l_sem, lres, lg_sem, 1)
    tokens = tsend[chip].astype(F32)
    for d in range(1, chips):
        t_copies[d - 1].wait_recv()
        tokens = tokens + trecv[d - 1].astype(F32)
    for s in range(samples):
        tok_out[s] = (tokens[s * slots : (s + 1) * slots] / divisor).astype(BF)

    for copy in sends:
        copy.wait_send()
    for unlike, copy in guarded:
        pl.when(unlike)(copy.wait_send)
    whole = gathered(eres, eg_sem)
    gtok_out[...] = whole[0:token_cols]
    shared(eres, eg_sem)
    whole = gathered(lres, lg_sem)
    gproj_out[0] = whole[0:depth]
    gproj_out[1] = whole[depth : 2 * depth]
    gproj_out[3] = whole[2 * depth : 3 * depth]
    gproj_out[2] = whole[3 * depth : 4 * depth]
    gout_out[...] = whole[4 * depth : 5 * depth]
    pair_row = whole[5 * depth : 5 * depth + 1]
    channel_of = lax.rem(iota((channels, width), 1), channels) == iota((channels, width), 0)
    pair_col = jnp.sum(jnp.where(channel_of, pair_row, 0.0), axis=1, keepdims=True)
    across = iota((channels, width), 0) == iota((channels, width), 1)
    pair_row = jnp.sum(jnp.where(across, pair_col, 0.0), axis=0, keepdims=True)
    gpair_out[...] = pair_row[:, :channels]
    shared(lres, lg_sem)


def on_device(atom_feats, pair_feats, tok_slot, w_proj, w_out, w_pair, w_tok, d_tok):
    samples, atoms, width = atom_feats.shape
    depth = w_proj.shape[2]
    slots, token_cols = d_tok.shape[1], d_tok.shape[2]
    channels = w_pair.shape[0]
    n = lax.axis_size("slab")
    heads = lax.axis_size("head")
    chips = heads // CORES
    own_atoms = atoms // chips
    blocks = own_atoms // Q_WIN
    rows = samples * own_atoms
    stack = chips * Q_WIN
    flat = Q_WIN * channels
    columns = chips * token_cols
    inner = next(m for m in (8, 4, 2, 1) if n % m == 0)
    outer = n // inner
    reducers = inner // 2 if inner > 2 else inner
    e_piece = -(-token_cols // (16 * reducers)) * 16
    l_piece = -(-(5 * depth + 8) // (16 * reducers)) * 16
    far = max(outer - 1, 1)

    def vm(*shape, dtype=BF):
        return pltpu.VMEM(shape, dtype)

    def sems(*shape):
        return pltpu.SemaphoreType.DMA((2,) + shape)

    scratch = [
        vm(samples, atoms + 2 * RIM, width),
        vm(flat, blocks * K_WIN),
        vm(1, atoms, dtype=jnp.int32),
        vm(1, own_atoms, dtype=jnp.int32),
        vm(4, chips, depth, width),
        vm(CORES, chips, depth, width),
        vm(chips, 1, channels),
        vm(chips, token_cols, width),
        vm(chips, samples, slots, token_cols),
        vm(samples, own_atoms + 2 * RIM, 2 * width),
        vm(stack, blocks * K_WIN, dtype=F32),
        vm(stack, flat),
        vm(rows, width),
        vm(rows, width, dtype=F32),
        vm(samples * blocks, stack, K_WIN, dtype=F32),
        vm(rows, chips * width),
        vm(rows, width, dtype=F32),
        vm(rows, 2 * width),
        vm(2 * width, width),
        vm(rows, width),
        vm(rows, columns),
        vm(rows, columns),
        vm(rows, columns),
        vm(rows, width),
        vm(rows, width),
        vm(rows, width),
        vm(rows, width),
        vm(rows, width),
        vm(rows, chips * width),
        vm(stack, blocks * K_WIN),
        vm(chips, samples * slots, token_cols),
        vm(max(chips - 1, 1), samples * slots, token_cols),
        vm(chips, reducers, e_piece, width),
        vm(chips, inner, e_piece, width),
        vm(reducers, e_piece, width),
        vm(chips, reducers, l_piece, width),
        vm(chips, inner, l_piece, width),
        vm(reducers, l_piece, width),
        vm(2, outer, max(e_piece, l_piece), width),
        pltpu.SemaphoreType.DMA((8,)),
        pltpu.SemaphoreType.DMA((blocks,)),
        sems(4, max(chips - 1, 1)),
        sems(heads - 1),
        sems(2),
        sems(samples),
        sems(samples),
        sems(max(chips - 1, 1)),
        sems(chips, inner),
        sems(inner),
        sems(chips, inner),
        sems(inner),
        sems(2, far),
    ]
    in_vmem = pl.BlockSpec(memory_space=pltpu.VMEM)
    in_hbm = pl.BlockSpec(memory_space=pltpu.HBM)
    shapes = (
        jax.ShapeDtypeStruct((samples, slots, token_cols), BF),
        jax.ShapeDtypeStruct((4, depth, width), F32),
        jax.ShapeDtypeStruct((depth, width), F32),
        jax.ShapeDtypeStruct((1, channels), F32),
        jax.ShapeDtypeStruct((token_cols, width), F32),
    )
    results = pl.pallas_call(
        functools.partial(kernel, n, heads, inner),
        out_shape=shapes,
        in_specs=[in_hbm] * 8,
        out_specs=[in_vmem] * 5,
        scratch_shapes=scratch,
        compiler_params=pltpu.CompilerParams(
            collective_id=0, has_side_effects=True, vmem_limit_bytes=67043328
        ),
    )(
        atom_feats,
        pair_feats.reshape(atoms * channels, K_WIN),
        tok_slot.reshape(1, atoms),
        jnp.swapaxes(w_proj, 1, 2),
        w_out,
        w_pair.T,
        w_tok.T,
        d_tok,
    )
    tok_act, grad_proj, grad_out, grad_pair, grad_tok = pl.pallas_call(
        store,
        out_shape=shapes,
        in_specs=[in_vmem] * 5,
        out_specs=[in_hbm] * 5,
        scratch_shapes=[pltpu.SemaphoreType.DMA((5,))],
    )(*results)
    return tok_act, jnp.swapaxes(grad_proj, 1, 2), grad_out, grad_pair.T, grad_tok.T


def store(*refs):
    sem = refs[10]
    copies = [pltpu.make_async_copy(refs[i], refs[5 + i], sem.at[i]) for i in range(5)]
    for copy in copies:
        copy.start()
    for copy in copies:
        copy.wait()


def solution(mesh):
    return jax.shard_map(
        on_device,
        mesh=mesh,
        in_specs=(
            P(None, "slab", None),
            P("slab", None, None),
            P("slab"),
            P(None, None, "head"),
            P("head", None),
            P(None, "head"),
            P(None, "head"),
            P(None, "slab", "head"),
        ),
        out_specs=(
            P(None, "slab", "head"),
            P(None, None, "head"),
            P("head", None),
            P(None, "head"),
            P(None, "head"),
        ),
        check_vma=False,
    )
```

```python
import functools
import jax
import jax.numpy as jnp
from jax import lax
from jax.experimental import pallas as pl
from jax.experimental.pallas import tpu as pltpu
from jax.sharding import PartitionSpec as P

Q_WIN = 32
K_WIN = 128
RIM = 48
CORES = 2
GROUP = 8
EPSILON = 1e-05
MASKED = -1e30
BF = jnp.bfloat16
F32 = jnp.float32
NT = (((1,), (1,)), ((), ()))
NN = (((1,), (0,)), ((), ()))
TN = (((0,), (0,)), ((), ()))


def mm(a, b, dims=NN):
    return lax.dot_general(a, b, dims, preferred_element_type=F32)


def iota(shape, dim):
    return lax.broadcasted_iota(jnp.int32, shape, dim)


def layer_norm(x):
    x = x.astype(F32)
    centered = x - jnp.mean(x, axis=-1, keepdims=True)
    variance = jnp.mean(centered * centered, axis=-1, keepdims=True)
    return (centered * lax.rsqrt(variance + EPSILON)).astype(BF)


def kernel(
    n, heads, inner,
    feats_in, pair_in, slot_in, wproj_in, wout_in, wpair_in, wtok_in, dtok_in,
    tok_out, gproj_out, gout_out, gpair_out, gtok_out,
    fx, pair, slot, slot_own, wproj, wout, wpair, wtok, dtok,
    keyed, bias, mixer, queries, gate, prob, zcat, att, hcat, wcat, half, spread, acts, ags, mgs, mgr, mg, attg, qg, ycat, dcat,
    tsend, trecv, ebuf, erecv, eres, lbuf, lrecv, lres, xbuf,
    in_sem, pair_sem, w_sem, wo_sem, halo_sem, h_sem, m_sem, t_sem, e_sem, eg_sem, l_sem, lg_sem, x_sem,
):
    samples = fx.shape[0]
    width = fx.shape[2]
    atoms = fx.shape[1] - 2 * RIM
    chips, depth = wproj.shape[1], wproj.shape[2]
    side = chips * depth
    own_atoms = atoms // chips
    blocks = own_atoms // Q_WIN
    slots, token_cols = dtok.shape[2], dtok.shape[3]
    channels = wpair.shape[2]
    flat = Q_WIN * channels
    stack = chips * Q_WIN
    scale = depth ** (-0.5)
    factor = (samples * atoms * n) ** (-0.5)
    outer = n // inner
    me_s = lax.axis_index("slab")
    me_h = lax.axis_index("head")
    own = lax.rem(me_s, inner)
    base = me_s - own
    far_own = me_s // inner
    core = lax.rem(me_h, CORES)
    chip = me_h // CORES
    partner = {"head": me_h + 1 - 2 * core}
    reducers = ebuf.shape[1]
    first_reducer = (inner - reducers) // 2
    sends = []
    guarded = []

    def head_peer(k):
        return {"head": lax.rem(me_h + k, heads)}

    def chip_peer(d):
        return {"head": lax.rem(chip + d, chips) * CORES + core}

    def inner_peer(k):
        return {"slab": base + lax.rem(own + k, inner)}

    def block_peer(d, k):
        return {"slab": base + lax.rem(own + k, inner), "head": lax.rem(chip + d, chips) * CORES + core}

    def outer_peer(k):
        return {"slab": lax.rem(me_s + k * inner, n)}

    def ring_peer(k):
        return {"slab": lax.rem(me_s + k + n, n)}

    def send(src, dst, sems, index, device):
        copy = pltpu.make_async_remote_copy(
            src_ref=src, dst_ref=dst, send_sem=sems.at[(0,) + index], recv_sem=sems.at[(1,) + index],
            device_id=device, device_id_type=pl.DeviceIdType.MESH,
        )
        copy.start()
        sends.append(copy)
        return copy

    def arrive(copies):
        for copy in copies:
            copy.wait_recv()

    greeted = [head_peer(k) for k in range(1, heads)] + [inner_peer(k) for k in range(1, inner)]
    greeted += [block_peer(d, k) for d in range(1, chips) for k in range(1, inner)]
    greeted += [outer_peer(k) for k in range(1, outer)]
    if outer > 1:
        greeted += [ring_peer(1), ring_peer(-1)]
    barrier = pltpu.get_barrier_semaphore()
    for device in greeted:
        pl.semaphore_signal(barrier, inc=1, device_id=device, device_id_type=pl.DeviceIdType.MESH)

    first_atom = pl.multiple_of(chip * own_atoms, own_atoms)
    loads = [
        pltpu.make_async_copy(a, b, in_sem.at[i])
        for i, (a, b) in enumerate(
            [
                (feats_in, fx.at[:, RIM : RIM + atoms, :]),
                (wproj_in, wproj.at[:, chip]),
                (wout_in, wout.at[core, chip]),
                (slot_in, slot),
                (slot_in.at[:, pl.ds(first_atom, own_atoms)], slot_own),
                (dtok_in, dtok.at[chip]),
                (wpair_in, wpair.at[chip]),
                (wtok_in, wtok.at[chip]),
            ]
        )
    ]
    pair_loads = [
        pltpu.make_async_copy(
            pair_in.at[pl.ds(pl.multiple_of(first_atom * channels, flat) + b * flat, flat), :],
            pair.at[:, b * K_WIN : (b + 1) * K_WIN],
            pair_sem.at[b],
        )
        for b in range(blocks)
    ]
    for load in loads + pair_loads:
        load.start()

    pl.semaphore_wait(barrier, len(greeted))

    def share_far(i, src, dst):
        return [send(src, dst, w_sem, (i, d - 1), chip_peer(d)) for d in range(1, chips)]

    wpair_copies = share_far(1, wpair_in, wpair.at[chip])
    wproj_copies = share_far(0, wproj_in, wproj.at[:, chip])
    to_left = send(
        feats_in.at[:, 0:RIM, :], fx.at[:, RIM + atoms : RIM + atoms + RIM, :], halo_sem, (1,), ring_peer(-1)
    )
    to_right = send(feats_in.at[:, atoms - RIM : atoms, :], fx.at[:, 0:RIM, :], halo_sem, (0,), ring_peer(1))
    wout_copies = [send(wout_in, wout.at[core, chip], wo_sem, (k - 1,), head_peer(k)) for k in range(1, heads)]
    wtok_copies = share_far(2, wtok_in, wtok.at[chip])
    dtok_copies = share_far(3, dtok_in, dtok.at[chip])

    lane_group = iota((Q_WIN, width), 1) // depth

    def masked_stack(wide, first):
        wide = wide.astype(F32)
        parts = [jnp.where(lane_group == first + h, wide, 0.0) for h in range(chips)]
        return jnp.concatenate(parts, axis=0).astype(BF)

    def diagonal_pick(tall):
        out = tall[0:Q_WIN]
        for h in range(1, chips):
            out = jnp.where(lax.rem(lane_group, chips) == h, tall[h * Q_WIN : (h + 1) * Q_WIN], out)
        return out

    def feats_rows(s, start, size):
        return fx[s, pl.ds(first_atom + start, size), :]

    def sample(s):
        return slice(s * own_atoms, (s + 1) * own_atoms)

    loads[0].wait()
    for s in range(samples):
        keyed[s, RIM : RIM + own_atoms, width : 2 * width] = layer_norm(feats_rows(s, RIM, own_atoms))

    loads[3].wait()
    loads[4].wait()
    slot_ids = me_s * slots
    member = jnp.where(slot[...] == slot_ids + iota((slots, atoms), 0), 1.0, 0.0)
    divisor = jnp.maximum(jnp.sum(member, axis=1, keepdims=True), 1.0)
    member = jnp.where(slot_own[...] == slot_ids + iota((slots, own_atoms), 0), 1.0, 0.0).astype(BF)

    loads[6].wait()
    arrive(wpair_copies)
    picker = lax.rem(iota((channels, flat), 1), channels) == iota((channels, flat), 0)
    w_tall = jnp.concatenate(
        [jnp.broadcast_to(wpair[h].astype(F32), (Q_WIN, channels)) for h in range(chips)], axis=0
    ).astype(BF)
    w_rows = mm(w_tall, picker.astype(F32).astype(BF))
    diagonal = iota((stack, flat), 1) // channels == lax.rem(iota((stack, flat), 0), Q_WIN)
    mixer[...] = jnp.where(diagonal, w_rows, 0.0).astype(BF)
    for load in pair_loads:
        load.wait()
    block_start = (me_s * chips + chip) * own_atoms - RIM
    reach = K_WIN - Q_WIN - RIM
    for b in range(blocks):
        cols = slice(b * K_WIN, (b + 1) * K_WIN)
        bias[:, cols] = mm(mixer[...], pair[:, cols])
        if b * Q_WIN < RIM or (b + 1) * Q_WIN + reach > own_atoms:
            where = block_start + b * Q_WIN + iota((stack, K_WIN), 1)
            bias[:, cols] = jnp.where((where >= 0) & (where < atoms * n), bias[:, cols], MASKED)

    loads[1].wait()
    arrive(wproj_copies)
    query_gate = jnp.concatenate([wproj[0].reshape(side, width), wproj[3].reshape(side, width)], axis=0)
    key_value = wproj[1:3].reshape(2 * side, width)
    def project(s):
        projected = mm(keyed[s, RIM : RIM + own_atoms, width : 2 * width], query_gate, NT)
        queries[sample(s), :] = (projected * scale).astype(BF)
        gate[sample(s), :] = jax.nn.sigmoid(projected)

        for start in (0, RIM + own_atoms):
            keyed[s, start : start + RIM, width : 2 * width] = layer_norm(feats_rows(s, start, RIM))
        keyed[s, :, 0:width] = mm(keyed[s, :, width : 2 * width], key_value, NT).astype(BF)

    to_right.wait_recv()
    to_left.wait_recv()
    def tile(s, b):
        return slice(s * own_atoms + b * Q_WIN, s * own_atoms + (b + 1) * Q_WIN)

    def window(s, b, wide):
        return keyed[s, b * Q_WIN : b * Q_WIN + K_WIN, 0 : wide * width]

    def forward(s, group):
        raw = [
            mm(masked_stack(queries[tile(s, b), :], 0), window(s, b, 1), NT) + bias[:, b * K_WIN : (b + 1) * K_WIN]
            for b in group
        ]
        tops = [jnp.max(scores, axis=1, keepdims=True) for scores in raw]
        powers = [jnp.exp(scores - top) for scores, top in zip(raw, tops)]
        sums = [jnp.sum(e, axis=1, keepdims=True) for e in powers]
        weights = [e * (1.0 / total) for e, total in zip(powers, sums)]
        for b, p in zip(group, weights):
            prob[s * blocks + b] = p
        results = [mm(p.astype(BF), window(s, b, 2)) for b, p in zip(group, weights)]
        for b, mixed_values in zip(group, results):
            at = tile(s, b)
            for h in range(chips):
                part = mixed_values[h * Q_WIN : (h + 1) * Q_WIN, width : 2 * width]
                zcat[at, h * width : (h + 1) * width] = part.astype(BF)
            attended = diagonal_pick(mixed_values[:, 0:width])
            att[at, :] = attended
            hcat[at, 0:width] = (gate[at, :] * attended).astype(BF)

    groups = [range(b, min(b + GROUP, blocks)) for b in range(0, blocks, GROUP)]

    h_copies = []
    for s in range(samples):
        project(s)
        for group in groups:
            forward(s, group)
        h_copies.append(send(hcat.at[sample(s), 0:width], hcat.at[sample(s), width : 2 * width], h_sem, (s,), partner))

    loads[2].wait()
    arrive(wout_copies)
    blank = jnp.zeros((side, width), BF)
    wcat[0:side, :] = blank
    wcat[side : 2 * side, :] = wout[core].reshape(side, width)
    wcat[2 * side : 3 * side, :] = blank
    wcat[3 * side : 4 * side, :] = wout[1 - core].reshape(side, width)
    loads[7].wait()
    arrive(wtok_copies)
    w_tok = wtok.reshape(chips * token_cols, width)
    loads[5].wait()
    arrive(dtok_copies)
    def spread_tokens(s):
        wide = jnp.concatenate([dtok[h, s].astype(F32) for h in range(chips)], axis=1)
        spread[sample(s), :] = mm(member, (wide / divisor).astype(BF), TN).astype(BF)

    m_copies = []
    span = 2 * width
    columns = chips * token_cols
    def middle(s):
        at = sample(s)
        h_copies[s].wait_recv()
        mixed = feats_rows(s, RIM, own_atoms).astype(F32) + mm(hcat[at, :], wcat[...])
        half[at, :] = mixed.astype(BF)
        total = None
        for start in range(0, columns, span):
            cols = slice(start, min(start + span, columns))
            pre = mm(half[at, :], w_tok[cols, :], NT)
            g1 = jax.nn.sigmoid(pre)
            acts[at, cols] = (pre * g1).astype(BF)
            ag = (spread[at, cols].astype(F32) * (g1 * (1.0 + pre * (1.0 - g1)))).astype(BF)
            ags[at, cols] = ag
            term = mm(ag, w_tok[cols, :])
            total = term if total is None else total + term
        mgs[at, :] = total.astype(BF)
        m_copies.append(send(mgs.at[at], mgr.at[at], m_sem, (s,), partner))

    def token_sums(s):
        sums = mm(member, acts[sample(s), :])
        for h in range(chips):
            tsend[h, s * slots : (s + 1) * slots, :] = sums[:, h * token_cols : (h + 1) * token_cols].astype(BF)


    def before_backward(s):
        at = sample(s)
        m_copies[s].wait_recv()
        total = (mgs[at, :].astype(F32) + mgr[at, :].astype(F32)).astype(BF)
        mg[at, :] = total
        og = mm(total, wcat[0 : 2 * side, :], NT)
        gt = gate[at, :]
        attg[at, :] = (gt * og).astype(BF)
        qg[at, :] = (og * att[at, :] * gt * (1.0 - gt)).astype(BF)

    def backward(s, group):
        slopes = [mm(masked_stack(attg[tile(s, b), :], chips), window(s, b, 1), NT) for b in group]
        probs = [prob[s * blocks + b] for b in group]
        sums = [jnp.sum(p * dp, axis=1, keepdims=True) for p, dp in zip(probs, slopes)]
        grads = [(p * (dp - total)).astype(BF) for p, dp, total in zip(probs, slopes, sums)]
        results = [mm(ds, window(s, b, 2)) for b, ds in zip(group, grads)]
        for b, ds in zip(group, grads):
            cols = slice(b * K_WIN, (b + 1) * K_WIN)
            if s == 0:
                dcat[:, cols] = ds
            else:
                dcat[:, cols] = (dcat[:, cols].astype(F32) + ds.astype(F32)).astype(BF)
        for b, mixed_keys in zip(group, results):
            at = tile(s, b)
            query_grad = scale * diagonal_pick(mixed_keys[:, 0:width])
            qg[at, :] = jnp.where(lane_group < chips, query_grad, qg[at, :].astype(F32)).astype(BF)
            for h in range(chips):
                part = mixed_keys[h * Q_WIN : (h + 1) * Q_WIN, width : 2 * width]
                ycat[at, h * width : (h + 1) * width] = part.astype(BF)

    def head_block(a, h, first):
        return a[first + h * depth : first + (h + 1) * depth, h * width : (h + 1) * width]

    def pack(buf, h, parts):
        piece = buf.shape[2]
        spare = reducers * piece - sum(part.shape[0] for part in parts)
        if spare:
            parts = parts + [jnp.zeros((spare, width), F32)]
        packed = jnp.concatenate(parts, axis=0).astype(BF)
        for j in range(reducers):
            buf[h, j] = packed[j * piece : (j + 1) * piece]

    def scatter(buf, recv, sems):
        for d in reversed(range(chips)):
            for r in range(reducers):
                copy = pltpu.make_async_remote_copy(
                    src_ref=buf.at[lax.rem(chip + d, chips), r], dst_ref=recv.at[d, own],
                    send_sem=sems.at[0, d, r], recv_sem=sems.at[1, d, own],
                    device_id={"slab": base + first_reducer + r, "head": lax.rem(chip + d, chips) * CORES + core},
                    device_id_type=pl.DeviceIdType.MESH,
                )
                if d:
                    copy.start()
                    sends.append(copy)
                else:
                    pl.when(own != first_reducer + r)(copy.start)
                    guarded.append((own != first_reducer + r, copy))

    def reduce(buf, recv, sems, res, res_sems, where):
        mine = own - first_reducer

        @pl.when((own >= first_reducer) & (own < first_reducer + reducers))
        def _():
            recv[0, own] = buf[chip, mine]
            for d in range(chips):
                for i in range(inner):
                    copy = pltpu.make_async_remote_copy(
                        src_ref=buf.at[0, 0], dst_ref=recv.at[d, i], send_sem=sems.at[0, d, 0], recv_sem=sems.at[1, d, i],
                        device_id=inner_peer(1), device_id_type=pl.DeviceIdType.MESH,
                    )
                    if d:
                        copy.wait_recv()
                    else:
                        pl.when(own != i)(copy.wait_recv)
            total = None
            for d in range(chips):
                for i in range(inner):
                    term = recv[d, i].astype(F32)
                    total = term if total is None else total + term
            res[mine] = exchange_outer(total, where).astype(BF)
            for k in sorted(range(1, inner), key=lambda k: abs(2 * k - inner)):
                share(res, res_sems, k).start()

    def share(res, res_sems, k):
        mine = own - first_reducer
        return pltpu.make_async_remote_copy(
            src_ref=res.at[mine], dst_ref=res.at[mine], send_sem=res_sems.at[0, k - 1], recv_sem=res_sems.at[1, mine],
            device_id=inner_peer(k), device_id_type=pl.DeviceIdType.MESH,
        )

    def exchange_outer(value, where):
        if outer == 1:
            return value
        part = xbuf.at[where, far_own, pl.ds(0, value.shape[0])]
        part[...] = value.astype(BF)
        copies = [
            pltpu.make_async_remote_copy(
                src_ref=part, dst_ref=part, send_sem=x_sem.at[0, where, k - 1], recv_sem=x_sem.at[1, where, k - 1],
                device_id=outer_peer(k), device_id_type=pl.DeviceIdType.MESH,
            )
            for k in range(1, outer)
        ]
        for copy in copies:
            copy.start()
        for copy in copies:
            copy.wait()
        value = xbuf[where, 0, 0 : value.shape[0], :].astype(F32)
        for k in range(1, outer):
            value = value + xbuf[where, k, 0 : value.shape[0], :].astype(F32)
        return value

    def shared(res, res_sems):
        @pl.when((own >= first_reducer) & (own < first_reducer + reducers))
        def _():
            for k in range(1, inner):
                share(res, res_sems, k).wait_send()

    def gathered(res, res_sems):
        for r in range(reducers):
            copy = pltpu.make_async_remote_copy(
                src_ref=res.at[r], dst_ref=res.at[r], send_sem=res_sems.at[0, 0], recv_sem=res_sems.at[1, r],
                device_id=inner_peer(1), device_id_type=pl.DeviceIdType.MESH,
            )
            pl.when(own != first_reducer + r)(copy.wait_recv)
        return jnp.concatenate([res[r] for r in range(reducers)], axis=0).astype(F32) * factor

    gtok = None
    for s in range(samples):
        spread_tokens(s)
        middle(s)
        term = mm(ags[sample(s), :], half[sample(s), :], TN)
        gtok = term if gtok is None else gtok + term
    for h in range(chips):
        pack(ebuf, h, [gtok[h * token_cols : (h + 1) * token_cols]])
    scatter(ebuf, erecv, e_sem)

    for s in range(samples):
        before_backward(s)
        if s == samples - 1:
            gout = mm(hcat[:, 0:width], mg[...], TN)
            gvalue = mm(attg[...], zcat[...], TN)
        for group in groups:
            backward(s, group)
        normed = keyed[s, RIM : RIM + own_atoms, width : 2 * width]
        terms = (mm(qg[sample(s), :], normed, TN), mm(queries[sample(s), :], ycat[sample(s), :], TN))
        late = terms if s == 0 else [before + term for before, term in zip(late, terms)]

    gqg, gkey = late
    terms = jnp.where(diagonal, mm(dcat[...], pair[...], NT), 0.0)
    for h in range(chips):
        row = jnp.sum(terms[h * Q_WIN : (h + 1) * Q_WIN], axis=0, keepdims=True)
        folded = row[:, 0:width]
        for j in range(1, flat // width):
            folded = folded + row[:, j * width : (j + 1) * width]
        gates = gqg[side + h * depth : side + (h + 1) * depth]
        lines = [gqg[h * depth : (h + 1) * depth], head_block(gkey, h, 0), gates, head_block(gvalue, h, side)]
        lines += [gout[side + h * depth : side + (h + 1) * depth], jnp.broadcast_to(folded, (8, width))]
        pack(lbuf, h, lines)
    scatter(lbuf, lrecv, l_sem)
    for s in range(samples):
        token_sums(s)
    t_copies = [
        send(tsend.at[lax.rem(chip + d, chips)], trecv.at[d - 1], t_sem, (d - 1,), chip_peer(d)) for d in range(1, chips)
    ]

    reduce(ebuf, erecv, e_sem, eres, eg_sem, 0)
    reduce(lbuf, lrecv, l_sem, lres, lg_sem, 1)
    tokens = tsend[chip].astype(F32)
    for d in range(1, chips):
        t_copies[d - 1].wait_recv()
        tokens = tokens + trecv[d - 1].astype(F32)
    for s in range(samples):
        tok_out[s] = (tokens[s * slots : (s + 1) * slots] / divisor).astype(BF)

    for copy in sends:
        copy.wait_send()
    for unlike, copy in guarded:
        pl.when(unlike)(copy.wait_send)
    whole = gathered(eres, eg_sem)
    gtok_out[...] = whole[0:token_cols]
    shared(eres, eg_sem)
    whole = gathered(lres, lg_sem)
    gproj_out[0] = whole[0:depth]
    gproj_out[1] = whole[depth : 2 * depth]
    gproj_out[3] = whole[2 * depth : 3 * depth]
    gproj_out[2] = whole[3 * depth : 4 * depth]
    gout_out[...] = whole[4 * depth : 5 * depth]
    pair_row = whole[5 * depth : 5 * depth + 1]
    channel_of = lax.rem(iota((channels, width), 1), channels) == iota((channels, width), 0)
    pair_col = jnp.sum(jnp.where(channel_of, pair_row, 0.0), axis=1, keepdims=True)
    across = iota((channels, width), 0) == iota((channels, width), 1)
    pair_row = jnp.sum(jnp.where(across, pair_col, 0.0), axis=0, keepdims=True)
    gpair_out[...] = pair_row[:, :channels]
    shared(lres, lg_sem)


def on_device(atom_feats, pair_feats, tok_slot, w_proj, w_out, w_pair, w_tok, d_tok):
    samples, atoms, width = atom_feats.shape
    depth = w_proj.shape[2]
    slots, token_cols = d_tok.shape[1], d_tok.shape[2]
    channels = w_pair.shape[0]
    n = lax.axis_size("slab")
    heads = lax.axis_size("head")
    chips = heads // CORES
    own_atoms = atoms // chips
    blocks = own_atoms // Q_WIN
    rows = samples * own_atoms
    stack = chips * Q_WIN
    flat = Q_WIN * channels
    columns = chips * token_cols
    inner = next(m for m in (8, 4, 2, 1) if n % m == 0)
    outer = n // inner
    reducers = inner // 2 if inner > 2 else inner
    e_piece = -(-token_cols // (16 * reducers)) * 16
    l_piece = -(-(5 * depth + 8) // (16 * reducers)) * 16
    far = max(outer - 1, 1)

    def vm(*shape, dtype=BF):
        return pltpu.VMEM(shape, dtype)

    def sems(*shape):
        return pltpu.SemaphoreType.DMA((2,) + shape)

    scratch = [
        vm(samples, atoms + 2 * RIM, width),
        vm(flat, blocks * K_WIN),
        vm(1, atoms, dtype=jnp.int32),
        vm(1, own_atoms, dtype=jnp.int32),
        vm(4, chips, depth, width),
        vm(CORES, chips, depth, width),
        vm(chips, 1, channels),
        vm(chips, token_cols, width),
        vm(chips, samples, slots, token_cols),
        vm(samples, own_atoms + 2 * RIM, 2 * width),
        vm(stack, blocks * K_WIN, dtype=F32),
        vm(stack, flat),
        vm(rows, width),
        vm(rows, width, dtype=F32),
        vm(samples * blocks, stack, K_WIN, dtype=F32),
        vm(rows, chips * width),
        vm(rows, width, dtype=F32),
        vm(rows, 2 * width),
        vm(2 * width, width),
        vm(rows, width),
        vm(rows, columns),
        vm(rows, columns),
        vm(rows, columns),
        vm(rows, width),
        vm(rows, width),
        vm(rows, width),
        vm(rows, width),
        vm(rows, width),
        vm(rows, chips * width),
        vm(stack, blocks * K_WIN),
        vm(chips, samples * slots, token_cols),
        vm(max(chips - 1, 1), samples * slots, token_cols),
        vm(chips, reducers, e_piece, width),
        vm(chips, inner, e_piece, width),
        vm(reducers, e_piece, width),
        vm(chips, reducers, l_piece, width),
        vm(chips, inner, l_piece, width),
        vm(reducers, l_piece, width),
        vm(2, outer, max(e_piece, l_piece), width),
        pltpu.SemaphoreType.DMA((8,)),
        pltpu.SemaphoreType.DMA((blocks,)),
        sems(4, max(chips - 1, 1)),
        sems(heads - 1),
        sems(2),
        sems(samples),
        sems(samples),
        sems(max(chips - 1, 1)),
        sems(chips, inner),
        sems(inner),
        sems(chips, inner),
        sems(inner),
        sems(2, far),
    ]
    in_vmem = pl.BlockSpec(memory_space=pltpu.VMEM)
    in_hbm = pl.BlockSpec(memory_space=pltpu.HBM)
    shapes = (
        jax.ShapeDtypeStruct((samples, slots, token_cols), BF),
        jax.ShapeDtypeStruct((4, depth, width), F32),
        jax.ShapeDtypeStruct((depth, width), F32),
        jax.ShapeDtypeStruct((1, channels), F32),
        jax.ShapeDtypeStruct((token_cols, width), F32),
    )
    results = pl.pallas_call(
        functools.partial(kernel, n, heads, inner),
        out_shape=shapes,
        in_specs=[in_hbm] * 8,
        out_specs=[in_vmem] * 5,
        scratch_shapes=scratch,
        compiler_params=pltpu.CompilerParams(
            collective_id=0, has_side_effects=True, vmem_limit_bytes=67043328
        ),
    )(
        atom_feats,
        pair_feats.reshape(atoms * channels, K_WIN),
        tok_slot.reshape(1, atoms),
        jnp.swapaxes(w_proj, 1, 2),
        w_out,
        w_pair.T,
        w_tok.T,
        d_tok,
    )
    tok_act, grad_proj, grad_out, grad_pair, grad_tok = pl.pallas_call(
        store,
        out_shape=shapes,
        in_specs=[in_vmem] * 5,
        out_specs=[in_hbm] * 5,
        scratch_shapes=[pltpu.SemaphoreType.DMA((5,))],
    )(*results)
    return tok_act, jnp.swapaxes(grad_proj, 1, 2), grad_out, grad_pair.T, grad_tok.T


def store(*refs):
    sem = refs[10]
    copies = [pltpu.make_async_copy(refs[i], refs[5 + i], sem.at[i]) for i in range(5)]
    for copy in copies:
        copy.start()
    for copy in copies:
        copy.wait()


def solution(mesh):
    return jax.shard_map(
        on_device,
        mesh=mesh,
        in_specs=(
            P(None, "slab", None),
            P("slab", None, None),
            P("slab"),
            P(None, None, "head"),
            P("head", None),
            P(None, "head"),
            P(None, "head"),
            P(None, "slab", "head"),
        ),
        out_specs=(
            P(None, "slab", "head"),
            P(None, None, "head"),
            P("head", None),
            P(None, "head"),
            P(None, "head"),
        ),
        check_vma=False,
    )
```
